256 devices in a mesh: role: 4 (over y), atoms: 64 (over x, z, core).
Axes of the slice: x: 4, y: 4, z: 8, core: 2. Of those that a mesh axis runs over, the one named last changes fastest.
Arguments:
- features: bfloat16 [4, 64, 256, 256], P('role', 'atoms'), may hold values from -6 to 6
- positions: float32 [4, 64, 3, 256], P('role', 'atoms'), may hold values from 0 to 1, as said below
- neighbours: int32 [4, 64, 32, 256], P('role', 'atoms'), may hold values from 0 to 2304, as said below
- images: int32 [4, 64, 32, 256], P('role', 'atoms'), may hold values from 0 to 26
- wave: int32 [3, 2048], replicated, may hold values from -8 to 8, as said below
- kgain: float32 [256], replicated, may hold values from 0.5 to 4
- w_in: bfloat16 [256, 256], replicated, may hold values from -0.375 to 0.375
- w_query: bfloat16 [256, 256], replicated, may hold values from -0.375 to 0.375
- w_rbf: bfloat16 [64, 256], replicated, may hold values from -1.5 to 1.5
- b_rbf: float32 [256], replicated, may hold values from -4 to 4
- w_filter: bfloat16 [256, 256], replicated, may hold values from -0.375 to 0.375
- w_out: bfloat16 [256, 256], replicated, may hold values from -0.375 to 0.375
Outputs:
- updated: bfloat16 [4, 64, 256, 256], P('role', 'atoms')
The draws below stay inside these ranges and needn't reach their ends.
Inputs may be any that keep to these rules, and one draw needn't show every extreme that they name: `neighbours`: an entry (p * 3 + q) * 256 + t names atom t of the brick offset by p - 1 along the first and q - 1 along the second brick dimension, periodically; 2304 marks an empty slot. Empty slots come last; every list has 16 or more entries, and every brick has a full list. `positions`: atom coordinates of brick (a, b) lie in [a / 4, (a + 1) / 4) x [b / 64, (b + 1) / 64) x [0, 1). No wave vector has all three indices zero.
All inputs are finite; a program needn't handle non-finite values.
Results may differ from the reference program's by a relative error of at most 0.0085.
Values may be sent and summed in bfloat16 or wider, within the bound.
No kernel may reach another device: no remote copies, remote signals or barrier semaphores. Data moves between devices by JAX's collectives and lax.ppermute only.
A program may use at most 128 MiB of HBM per device.

```python
import math
import jax
import jax.numpy as jnp
from jax import lax

F = 256
KV = 2048
RBF = 64
NBR = 32
ATOMS_DEV = 256
BRX = 4
BRY = 64


def draw_positions(key, part):
    spread = jax.random.uniform(key, (BRX, BRY, 3, ATOMS_DEV), jnp.float32)
    first_cell = jnp.arange(BRX, dtype=jnp.float32)[:, None, None]
    second_cell = jnp.arange(BRY, dtype=jnp.float32)[None, :, None]
    first_coord = (first_cell + spread[:, :, 0]) / BRX
    second_coord = (second_cell + spread[:, :, 1]) / BRY
    third_coord = spread[:, :, 2]
    return jnp.stack([first_coord, second_coord, third_coord], axis=2).astype(jnp.float32)


def draw_neighbours(key, part):
    key_picks = jax.random.fold_in(key, 11)
    key_fill = jax.random.fold_in(key, 12)
    picks = jax.random.randint(key_picks, (BRX, BRY, NBR, ATOMS_DEV), 0, 9 * ATOMS_DEV)
    filled = jax.random.randint(key_fill, (BRX, BRY, 1, ATOMS_DEV), NBR // 2, NBR + 1)
    atom_index = jnp.arange(ATOMS_DEV, dtype=jnp.int32)[None, None, None, :]
    filled = jnp.where(atom_index == 0, NBR, filled)
    slot_index = jnp.arange(NBR, dtype=jnp.int32)[None, None, :, None]
    return jnp.where(slot_index < filled, picks, 9 * ATOMS_DEV).astype(jnp.int32)


def draw_wave(key, part):
    indices = jax.random.randint(key, (3, KV), -8, 9)
    all_zero = jnp.all(indices == 0, axis=0)
    first_row = jnp.where(all_zero, 1, indices[0])
    return jnp.concatenate([first_row[None, :], indices[1:]], axis=0).astype(jnp.int32)


def with_ends(values, rng, low, top_value):
    longest = values.shape.index(max(values.shape))
    spots = []
    for shift in (0, 1):
        where = [jax.random.randint(jax.random.fold_in(rng, axis), (), 0, length) for axis, length in enumerate(values.shape)]
        where[longest] = (where[longest] + shift) % values.shape[longest]
        spots.append(tuple(where))
    return values.at[spots[0]].set(low).at[spots[1]].set(top_value)


def block_levels(own_key, extent, cuts, low, high):
    loudness, own = 1.0, jax.random.fold_in(own_key, 6)
    for dim, parts in cuts:
        heights = jnp.exp(jax.random.uniform(jax.random.fold_in(own, dim), (parts,), jnp.float32, low / len(cuts), high / len(cuts)))
        loudness = loudness * jnp.repeat(heights, extent[dim] // parts).reshape([-1 if axis == dim else 1 for axis in range(len(extent))])
    return loudness


def centred(rng, shape, scale, reach, split=(), kind=jnp.bfloat16):
    array = jax.random.normal(rng, shape, jnp.float32) * scale
    if len(split) > 0:
        array = block_levels(rng, shape, split, -0.22, 0.18) * array
    return jnp.clip(array, min=-reach, max=reach).astype(kind)


def setup_inputs(seed: int = 0) -> dict:
    key_list = jax.random.split(jax.random.key(seed), 13)
    features = centred(key_list[0], (BRX, BRY, ATOMS_DEV, F), 1.0, 6.0, ((0, 4), (1, 64)))
    positions = draw_positions(jax.random.fold_in(key_list[12], 71), 0)
    neighbours = draw_neighbours(jax.random.fold_in(key_list[12], 71), 0)
    images = with_ends(jax.random.randint(key_list[3], (BRX, BRY, NBR, ATOMS_DEV), 0, 27), jax.random.fold_in(key_list[3], 1), 0, 26).astype(jnp.int32)
    wave = draw_wave(jax.random.fold_in(key_list[12], 71), 0)
    kgain = jnp.clip(jnp.exp(jax.random.uniform(key_list[5], (F,), jnp.float32, math.log(0.5), math.log(4.0))), 0.5, 4.0)
    w_in = centred(key_list[6], (F, F), F ** -0.5, 0.375)
    w_query = centred(key_list[7], (F, F), F ** -0.5, 0.375)
    w_rbf = centred(key_list[8], (RBF, F), (RBF // 4) ** -0.5, 1.5)
    b_rbf = centred(key_list[9], (F,), 1.0, 4.0, (), jnp.float32)
    w_filter = centred(key_list[10], (F, F), F ** -0.5, 0.375)
    w_out = centred(key_list[11], (F, F), F ** -0.5, 0.375)
    return dict(features=features, positions=positions, neighbours=neighbours, images=images, wave=wave, kgain=kgain, w_in=w_in, w_query=w_query, w_rbf=w_rbf, b_rbf=b_rbf, w_filter=w_filter, w_out=w_out)


box_side = 1.0
soft_sq = 0.01
damping = 64.0
ewald_scale = 0.25

def shifted_softplus(values):
    return jax.nn.softplus(values) - math.log(2.0)

def pair_messages(near_table, near_coords, own_pos, near_slots, near_images, w_rbf, b_rbf, w_filter):
    slot_count, atom_count = near_slots.shape
    flat_slots = near_slots.reshape(-1)
    near_pos = near_coords[:, flat_slots].reshape(3, slot_count, atom_count)
    offsets = jnp.stack([near_images // 9 - 1, near_images // 3 % 3 - 1, near_images % 3 - 1]).astype(jnp.float32) * box_side
    delta = near_pos + offsets - own_pos[:, None, :]
    distance = jnp.sqrt(lax.optimization_barrier(jnp.sum(delta * delta, axis=0)) + soft_sq)
    basis_count = w_rbf.shape[0]
    centers = jnp.arange(basis_count, dtype=jnp.float32) * (4.0 / (basis_count - 1))
    sharpness = (basis_count / 4.0) ** 2
    basis = jnp.exp(-sharpness * (distance.reshape(-1, 1) - centers[None, :]) ** 2).astype(jnp.bfloat16)
    inner = shifted_softplus(jnp.dot(basis, w_rbf, preferred_element_type=jnp.float32) + b_rbf).astype(jnp.bfloat16)
    filters = jnp.dot(inner, w_filter, preferred_element_type=jnp.float32)
    gathered = near_table[flat_slots].astype(jnp.float32)
    return (filters * gathered).reshape(slot_count, atom_count, -1).sum(axis=0)

def phase_tables(own_pos, wave):
    vectors = wave.astype(jnp.float32) * (2.0 * math.pi / box_side)
    angle = lax.dot_general(own_pos, vectors, (((0,), (0,)), ((), ())), precision=lax.Precision.HIGHEST)
    return (jnp.cos(angle).astype(jnp.bfloat16), jnp.sin(angle).astype(jnp.bfloat16))

def wave_filter(wave, kgain):
    squares = lax.optimization_barrier(jnp.sum(wave.astype(jnp.float32) ** 2, axis=0))
    return ewald_scale * kgain[None, :] * (jnp.exp(-squares / damping) / squares)[:, None]

def contract_rows(left_side, right_side):
    return lax.dot_general(left_side, right_side, (((0,), (0,)), ((), ())), preferred_element_type=jnp.float32)

def reference(features, positions, neighbours, images, wave, kgain, w_in, w_query, w_rbf, b_rbf, w_filter, w_out):
    brick_total = BRX * BRY
    feat_width = features.shape[3]
    atom_total = brick_total * ATOMS_DEV
    hidden_x = jnp.dot(features.reshape(-1, feat_width), w_in, preferred_element_type=jnp.float32).astype(jnp.bfloat16)
    hidden_x = hidden_x.reshape(BRX, BRY, ATOMS_DEV, feat_width)
    k_filter = wave_filter(wave, kgain)
    brick_ids = jnp.arange(brick_total, dtype=jnp.int32)

    def accumulate(running, brick):
        brick_x = brick // BRY
        brick_y = brick % BRY
        own_rows = features[brick_x, brick_y]
        queries = jnp.dot(own_rows, w_query, preferred_element_type=jnp.float32).astype(jnp.bfloat16)
        cosine, sine = phase_tables(positions[brick_x, brick_y], wave)
        partial_value = jnp.stack([contract_rows(cosine, queries), contract_rows(sine, queries)])
        return (running + partial_value * atom_total ** (-0.5), None)
    totals, _ = lax.scan(accumulate, jnp.zeros((2, KV, feat_width), jnp.float32), brick_ids)
    filtered = (totals * k_filter[None]).astype(jnp.bfloat16)

    def one_brick(brick):
        brick_x = brick // BRY
        brick_y = brick % BRY
        table_parts = []
        coord_parts = []
        for step_x in range(3):
            for step_y in range(3):
                other_x = (brick_x + step_x - 1) % BRX
                other_y = (brick_y + step_y - 1) % BRY
                table_parts.append(hidden_x[other_x, other_y])
                coord_parts.append(positions[other_x, other_y])
        table_parts.append(jnp.zeros((1, feat_width), jnp.bfloat16))
        coord_parts.append(jnp.zeros((3, 1), jnp.float32))
        near_table = jnp.concatenate(table_parts, axis=0)
        near_coords = jnp.concatenate(coord_parts, axis=1)
        own_pos = positions[brick_x, brick_y]
        short_msg = pair_messages(near_table, near_coords, own_pos, neighbours[brick_x, brick_y], images[brick_x, brick_y], w_rbf, b_rbf, w_filter)
        cosine, sine = phase_tables(own_pos, wave)
        ewald = jnp.dot(cosine, filtered[0], preferred_element_type=jnp.float32) + jnp.dot(sine, filtered[1], preferred_element_type=jnp.float32)
        combined = (short_msg * NBR ** (-0.5) + ewald).astype(jnp.bfloat16)
        own_rows = features[brick_x, brick_y]
        return (own_rows.astype(jnp.float32) + jnp.dot(combined, w_out, preferred_element_type=jnp.float32)).astype(jnp.bfloat16)
    result = lax.map(one_brick, brick_ids)
    return result.reshape(BRX, BRY, ATOMS_DEV, feat_width)
```

```python
import functools
import math

import jax
import jax.numpy as jnp
from jax import lax
from jax.experimental import pallas as pl
from jax.experimental.pallas import tpu as pltpu
from jax.sharding import PartitionSpec as P

box_side = 1.0
soft_sq = 0.01
damping = 64.0
ewald_scale = 0.25
SINE = (
    3.1415925800428712,
    -5.16770687881004,
    2.550031375353375,
    -0.5980451625033413,
    0.07722010591476362,
)
VMEM = pl.BlockSpec(memory_space=pltpu.VMEM)


def call(body, out, ins, scratch=(), flops=0, nbytes=0, trans=0, name=None):
    multiple = isinstance(out, (list, tuple))
    return pl.pallas_call(
        body,
        out_shape=out,
        in_specs=[VMEM] * len(ins),
        out_specs=[VMEM] * len(out) if multiple else VMEM,
        scratch_shapes=list(scratch),
        compiler_params=pltpu.CompilerParams(vmem_limit_bytes=48 << 20),
        cost_estimate=pl.CostEstimate(flops=flops, bytes_accessed=nbytes, transcendentals=trans),
        name=name,
    )(*ins)


def dot(left, right):
    return jnp.dot(left, right, preferred_element_type=jnp.float32)


def cos_turns(turns):
    rest = turns - jnp.round(turns)
    square = rest * rest
    poly = SINE[4]
    for coef in SINE[3::-1]:
        poly = poly * square + coef
    sine = poly * rest
    return 1.0 - 2.0 * (sine * sine)


def structure_kernel(scale, *refs):
    rows_refs, (pos_ref, wave_ref, wq_ref, out_ref, table, queries) = refs[:4], refs[4:]
    atoms = rows_refs[0].shape[0]
    weight = wq_ref[...]
    for i, rows in enumerate(rows_refs):
        queries[i * atoms : (i + 1) * atoms, :] = dot(rows[...], weight).astype(jnp.bfloat16)
    step = 128

    def block(j, carry):
        part = pl.ds(pl.multiple_of(j * step, step), step)
        waves = wave_ref[part, :]
        turns = (
            waves[:, 0:1] * pos_ref[0:1, :]
            + waves[:, 1:2] * pos_ref[1:2, :]
            + waves[:, 2:3] * pos_ref[2:3, :]
            - waves[:, 3:4]
        )
        table[part, :] = cos_turns(turns).astype(jnp.bfloat16)
        out_ref[part, :] = (dot(table[part, :], queries[...]) * scale).astype(jnp.bfloat16)
        return carry

    lax.fori_loop(0, wave_ref.shape[0] // step, block, 0)


def table_kernel(pos_ref, wave_ref, out_ref):
    step = 128

    def block(j, carry):
        part = pl.ds(pl.multiple_of(j * step, step), step)
        pos = pos_ref[part, :]
        turns = (
            pos[:, 0:1] * wave_ref[0:1, :]
            + pos[:, 1:2] * wave_ref[1:2, :]
            + pos[:, 2:3] * wave_ref[2:3, :]
            - wave_ref[3:4, :]
        )
        out_ref[part, :] = cos_turns(turns).astype(jnp.bfloat16)
        return carry

    lax.fori_loop(0, pos_ref.shape[0] // step, block, 0)


def ewald_kernel(table_ref, filtered_ref, out_ref):
    bricks, atoms, _ = out_ref.shape
    for i in range(bricks):
        part = table_ref[i * atoms : (i + 1) * atoms, :]
        out_ref[i] = dot(part, filtered_ref[...]).astype(jnp.bfloat16)


def final_kernel(rows_ref, short_ref, e0_ref, e1_ref, e2_ref, e3_ref, wout_ref, out_ref):
    total = short_ref[...]
    for ref in (e0_ref, e1_ref, e2_ref, e3_ref):
        total = total + ref[...].astype(jnp.float32)
    moved = dot(total.astype(jnp.bfloat16), wout_ref[...])
    out_ref[...] = (rows_ref[...].astype(jnp.float32) + moved).astype(jnp.bfloat16)


def short_kernel(scale, *refs):
    rows_refs = refs[:9]
    pos_ref, slots_ref, images_ref, own_ref, win_ref, wrbf_ref, brbf_ref, wf_ref = refs[9:17]
    out_ref, hidden, turned, dist_cols, brick_cols, atom_cols, hot = refs[17:]
    slots, atoms = slots_ref.shape
    basis_count = wrbf_ref.shape[0]
    width = wf_ref.shape[1]
    weight = win_ref[...]
    for i, rows in enumerate(rows_refs):
        hidden[i * atoms : (i + 1) * atoms, :] = dot(rows[...], weight).astype(jnp.bfloat16)
    zoom = (basis_count / 4.0) * math.sqrt(math.log2(math.e))
    lane = 128
    for half in range(atoms // lane):
        cut = slice(half * lane, (half + 1) * lane)
        index = slots_ref[:, cut]
        image = images_ref[:, cut]
        place = index & (lane - 1)
        group = index >> 7
        near = [jnp.zeros((slots, lane), jnp.float32) for _ in range(3)]
        for r in range(9 * atoms // lane):
            here = group == r
            for c in range(3):
                table = jnp.broadcast_to(
                    pos_ref[c : c + 1, r * lane : (r + 1) * lane], (slots, lane)
                )
                taken = jnp.take_along_axis(table, place, axis=1, mode="promise_in_bounds")
                near[c] = jnp.where(here, taken, near[c])
        first = (image >= 9).astype(jnp.int32) + (image >= 18).astype(jnp.int32)
        inside = image - 9 * first
        second = (inside >= 3).astype(jnp.int32) + (inside >= 6).astype(jnp.int32)
        third = inside - 3 * second
        square = jnp.zeros((slots, lane), jnp.float32)
        for c, offset in enumerate((first, second, third)):
            delta = near[c] + (offset - 1).astype(jnp.float32) * box_side - own_ref[c : c + 1, cut]
            square = square + delta * delta
        turned[0:slots, cut] = jnp.sqrt(square + soft_sq) * zoom
        turned[slots : 2 * slots, cut] = (index >> 8).astype(jnp.float32)
        turned[2 * slots : 3 * slots, cut] = (index & (atoms - 1)).astype(jnp.float32)
        turned[3 * slots : 4 * slots, cut] = jnp.zeros((slots, lane), jnp.float32)
    columns = turned[...].T
    low = lax.broadcasted_iota(jnp.int32, (atoms, lane), 1) < basis_count
    for s in range(slots):
        brick_cols[s] = jnp.broadcast_to(
            columns[:, slots + s : slots + s + 1], (atoms, lane)
        ).astype(jnp.bfloat16)
        atom_cols[s] = jnp.broadcast_to(
            columns[:, 2 * slots + s : 2 * slots + s + 1], (atoms, lane)
        ).astype(jnp.bfloat16)
    for j in range(slots // 2):
        dist_cols[j] = jnp.where(
            low,
            jnp.broadcast_to(columns[:, 2 * j : 2 * j + 1], (atoms, lane)),
            jnp.broadcast_to(columns[:, 2 * j + 1 : 2 * j + 2], (atoms, lane)),
        )
    out_ref[...] = jnp.zeros_like(out_ref)
    centers = (
        (lax.broadcasted_iota(jnp.int32, (1, lane), 1) & (basis_count - 1)).astype(jnp.float32)
        * (4.0 / (basis_count - 1))
        * zoom
    )
    numbers = lax.broadcasted_iota(jnp.int32, (atoms, lane), 1).astype(jnp.float32)
    one = jnp.ones((atoms, lane), jnp.bfloat16)
    zero = jnp.zeros((atoms, lane), jnp.bfloat16)
    numbers_low = numbers.astype(jnp.bfloat16)
    numbers_high = (numbers + float(lane)).astype(jnp.bfloat16)
    none = jnp.full((atoms, lane), -1.0, jnp.bfloat16)
    bias = brbf_ref[...]

    def pair(j, carry):
        offset = dist_cols[j] - centers
        basis = jnp.exp2(-(offset * offset)).astype(jnp.bfloat16)
        for k in range(2):
            s = 2 * j + k
            part = basis[:, k * basis_count : (k + 1) * basis_count]
            value = dot(part, wrbf_ref[...]) + bias
            inner = (jnp.log(1.0 + jnp.exp(value)) - math.log(2.0)).astype(jnp.bfloat16)
            filters = dot(inner, wf_ref[...])
            brick = brick_cols[s]
            atom = atom_cols[s]
            for b in range(9):
                mine = jnp.where(brick == jnp.bfloat16(b), atom, none)
                hot[:, b * atoms : b * atoms + lane] = jnp.where(mine == numbers_low, one, zero)
                hot[:, b * atoms + lane : (b + 1) * atoms] = jnp.where(
                    mine == numbers_high, one, zero
                )
            gathered = dot(hot[...], hidden[...])
            out_ref[...] += filters * gathered
        return carry

    lax.fori_loop(0, slots // 2, pair, 0)
    out_ref[...] = out_ref[...] * scale


def local(
    features,
    positions,
    neighbours,
    images,
    wave,
    kgain,
    w_in,
    w_query,
    w_rbf,
    b_rbf,
    w_filter,
    w_out,
):
    f32, bf16 = jnp.float32, jnp.bfloat16
    rows = features[0, 0]
    place = positions[0, 0]
    atoms, width = rows.shape
    slots = neighbours.shape[2]
    roles = lax.axis_size("role")
    columns = lax.axis_size("atoms")
    atom_total = atoms * roles * columns
    waves = wave.shape[1]
    share = waves // roles
    piece = share // columns
    role = lax.axis_index("role")
    column = lax.axis_index("atoms")

    def from_role(block, shift):
        return lax.ppermute(block, "role", [((i + shift) % roles, i) for i in range(roles)])

    def from_column(block, shift):
        return lax.ppermute(
            block, "atoms", [((i + shift) % columns, i) for i in range(columns)]
        )

    shifts = (1, roles - 1, 2)
    place_of = {0: place, **{d: from_role(place, d) for d in shifts}}
    rows_of = {0: rows, **{d: from_role(rows, d) for d in shifts}}
    order = (0,) + shifts

    own_waves = lax.dynamic_slice_in_dim(wave, role * share, share, axis=1).astype(f32)
    phase = jnp.broadcast_to(
        jnp.asarray([0.0, 0.25], f32)[None, None, :, None], (1, columns, 2, piece)
    ).reshape(1, 2 * share)
    doubled = jnp.broadcast_to(
        own_waves.reshape(3, columns, 1, piece), (3, columns, 2, piece)
    ).reshape(3, 2 * share)
    wave_rows = jnp.concatenate([doubled, phase], axis=0)
    wave_cols = wave_rows.T
    group_pos = jnp.concatenate([place_of[d] for d in order], axis=1)

    partial = call(
        functools.partial(structure_kernel, atom_total ** (-0.5)),
        jax.ShapeDtypeStruct((2 * share, width), bf16),
        [rows_of[d] for d in order] + [group_pos, wave_cols, w_query],
        scratch=[
            pltpu.VMEM((2 * share, roles * atoms), bf16),
            pltpu.VMEM((roles * atoms, width), bf16),
        ],
        flops=2 * 2 * share * roles * atoms * width,
        nbytes=4 << 20,
        name="structure",
    )
    chunks = partial.reshape(columns, 2 * piece, width)
    mine = lax.all_to_all(chunks, "atoms", 0, 0)
    total = jnp.sum(mine.astype(f32), axis=0)

    my_waves = lax.dynamic_slice_in_dim(
        wave, role * share + column * piece, piece, axis=1
    ).astype(f32)
    squares = jnp.sum(my_waves * my_waves, axis=0)
    k_filter = ewald_scale * kgain[None, :] * (jnp.exp(-squares / damping) / squares)[:, None]
    filtered = (total.reshape(2, piece, width) * k_filter[None]).astype(bf16)
    copies = jnp.broadcast_to(
        filtered.reshape(1, 2 * piece, width), (columns, 2 * piece, width)
    )
    everyone = lax.all_to_all(copies, "atoms", 0, 0).reshape(2 * share, width)

    near_rows = {}
    near_pos = {}
    triple = (roles - 1, 0, 1)
    stack_rows = jnp.stack([rows_of[d] for d in triple])
    stack_pos = jnp.stack([place_of[d] for d in triple])
    for q, step in ((0, columns - 1), (2, 1)):
        got_rows = from_column(stack_rows, step)
        got_pos = from_column(stack_pos, step)
        for p in range(3):
            near_rows[p, q] = got_rows[p]
            near_pos[p, q] = got_pos[p]
    for p, d in enumerate(triple):
        near_rows[p, 1] = rows_of[d]
        near_pos[p, 1] = place_of[d]
    window = [(p, q) for p in range(3) for q in range(3)]
    near_table = jnp.concatenate([near_pos[w] for w in window], axis=1)
    short = call(
        functools.partial(short_kernel, slots ** (-0.5)),
        jax.ShapeDtypeStruct((atoms, width), f32),
        [near_rows[w] for w in window]
        + [
            near_table,
            neighbours[0, 0],
            images[0, 0],
            place,
            w_in,
            w_rbf,
            b_rbf[None, :],
            w_filter,
        ],
        scratch=[
            pltpu.VMEM((9 * atoms, width), bf16),
            pltpu.VMEM((4 * slots, atoms), f32),
            pltpu.VMEM((slots // 2, atoms, 128), f32),
            pltpu.VMEM((slots, atoms, 128), bf16),
            pltpu.VMEM((slots, atoms, 128), bf16),
            pltpu.VMEM((atoms, 9 * atoms), bf16),
        ],
        flops=2 * slots * atoms * 9 * atoms * width,
        nbytes=4 << 20,
        name="short",
    )
    table = call(
        table_kernel,
        jax.ShapeDtypeStruct((roles * atoms, 2 * share), bf16),
        [group_pos.T, wave_rows],
        nbytes=4 << 20,
        name="table",
    )
    parts = call(
        ewald_kernel,
        jax.ShapeDtypeStruct((roles, atoms, width), bf16),
        [table, everyone],
        flops=2 * 2 * share * roles * atoms * width,
        nbytes=4 << 20,
        name="ewald",
    )
    back = [parts[0]] + [from_role(parts[1 + i], roles - d) for i, d in enumerate(shifts)]
    result = call(
        final_kernel,
        jax.ShapeDtypeStruct((atoms, width), bf16),
        [rows, short] + back + [w_out],
        flops=2 * atoms * width * width,
        nbytes=1 << 20,
        name="final",
    )
    return result[None, None]


def solution(mesh):
    in_specs = (
        P("role", "atoms", None, None),
        P("role", "atoms", None, None),
        P("role", "atoms", None, None),
        P("role", "atoms", None, None),
        P(),
        P(),
        P(),
        P(),
        P(),
        P(),
        P(),
        P(),
    )
    out_specs = P("role", "atoms", None, None)
    return jax.shard_map(local, mesh=mesh, in_specs=in_specs, out_specs=out_specs, check_vma=False)
```

```python
import functools
import math

import jax
import jax.numpy as jnp
from jax import lax
from jax.experimental import pallas as pl
from jax.experimental.pallas import tpu as pltpu
from jax.sharding import PartitionSpec as P

box_side = 1.0
soft_sq = 0.01
damping = 64.0
ewald_scale = 0.25
SINE = (
    3.1415925800428712,
    -5.16770687881004,
    2.550031375353375,
    -0.5980451625033413,
    0.07722010591476362,
)
COSINE = (
    0.9999999534655706,
    -4.934792858503339,
    4.058411910098915,
    -1.331880131184001,
    0.21969673041819898,
)
ZOOM = 16.0 * math.sqrt(math.log2(math.e))
VMEM = pl.BlockSpec(memory_space=pltpu.VMEM)


def call(body, out, ins, scratch=(), flops=0, nbytes=0, trans=0, name=None):
    multiple = isinstance(out, (list, tuple))
    return pl.pallas_call(
        body,
        out_shape=out,
        in_specs=[VMEM] * len(ins),
        out_specs=[VMEM] * len(out) if multiple else VMEM,
        scratch_shapes=list(scratch),
        compiler_params=pltpu.CompilerParams(vmem_limit_bytes=48 << 20),
        cost_estimate=pl.CostEstimate(flops=flops, bytes_accessed=nbytes, transcendentals=trans),
        name=name,
    )(*ins)


def dot(left, right):
    return jnp.dot(left, right, preferred_element_type=jnp.float32)


def sine_cosine(turns):
    rest = turns - jnp.round(turns)
    square = rest * rest
    odd = SINE[-1]
    for coef in SINE[-2::-1]:
        odd = odd * square + coef
    even = COSINE[-1]
    for coef in COSINE[-2::-1]:
        even = even * square + coef
    half = odd * rest
    return 2.0 * (half * even), 1.0 - 2.0 * (half * half)


def tables_kernel(*refs):
    pos_refs, (wave_ref, by_wave, by_atom, pos, cols) = refs[:4], refs[4:]
    atoms = pos_refs[0].shape[1]
    for i, ref in enumerate(pos_refs):
        pos[:, i * atoms : (i + 1) * atoms] = ref[...]
    share = by_wave.shape[0] // 2
    role = lax.axis_index("role")
    for i in range(share // 128):
        first = pl.multiple_of(role * share + i * 128, 128)
        cols[i * 128 : (i + 1) * 128, 0:3] = wave_ref[:, pl.ds(first, 128)].astype(jnp.float32).T
    step = 64
    total = pos.shape[1]

    def block(j, carry):
        waves = cols[pl.ds(pl.multiple_of(j * step, step), step), :]
        turns = (
            waves[:, 0:1] * pos[0:1, :] + waves[:, 1:2] * pos[1:2, :] + waves[:, 2:3] * pos[2:3, :]
        )
        sine, cosine = sine_cosine(turns)
        both = jnp.stack(
            [cosine.reshape(step // 8, 8, total), sine.reshape(step // 8, 8, total)], axis=1
        ).reshape(2 * step, total)
        part = pl.ds(pl.multiple_of(j * 2 * step, 2 * step), 2 * step)
        by_wave[part, :] = both.astype(jnp.bfloat16)
        by_atom[:, part] = both.T.astype(jnp.bfloat16)
        return carry

    lax.fori_loop(0, share // step, block, 0)


def structure_kernel(scale, *refs):
    rows_refs, (wq_ref, table, out_ref, queries) = refs[:4], refs[4:]
    atoms = rows_refs[0].shape[0]
    weight = wq_ref[...]
    for i, rows in enumerate(rows_refs):
        queries[i * atoms : (i + 1) * atoms, :] = dot(rows[...], weight).astype(jnp.bfloat16)
    out_ref[...] = (dot(table[...], queries[...]) * scale).astype(jnp.bfloat16)


def stack_kernel(*refs):
    rows_refs, pos_refs, (out_ref, parts) = refs[:3], refs[3:6], refs[6:]
    atoms = rows_refs[0].shape[0]
    parts[...] = jnp.zeros_like(parts)
    for i in range(3):
        out_ref[i, 0:atoms, :] = rows_refs[i][...]
        rest = pos_refs[i][...]
        for k in range(3):
            rounded = rest.astype(jnp.bfloat16).astype(jnp.float32)
            parts[8 * k : 8 * k + 3, :] = rounded
            rest = rest - rounded
        out_ref[i, atoms:, :] = parts[...].astype(jnp.bfloat16)


def reduce_kernel(mine_ref, wave_ref, kgain_ref, out_ref):
    columns, rows, width = mine_ref.shape
    piece = rows // 2
    share = columns * piece
    first = lax.axis_index("role") * share + lax.axis_index("atoms") * piece
    start = pl.multiple_of((first // 128) * 128, 128)
    waves = wave_ref[:, pl.ds(start, 128)].astype(jnp.float32)
    squares = jnp.broadcast_to(jnp.sum(waves * waves, axis=0, keepdims=True), (piece, 128))
    lanes = lax.broadcasted_iota(jnp.int32, (piece, 128), 1)
    wanted = lax.broadcasted_iota(jnp.int32, (piece, 128), 0) + (first - start)
    square = jnp.sum(jnp.where(lanes == wanted, squares, 0.0), axis=1, keepdims=True)
    k_filter = ewald_scale * kgain_ref[...] * (jnp.exp(-square / damping) / square)
    total = jnp.sum(mine_ref[...].astype(jnp.float32), axis=0)
    filtered = total * jnp.concatenate([k_filter, k_filter], axis=0)
    out_ref[...] = jnp.broadcast_to(filtered.astype(jnp.bfloat16)[None], (columns, rows, width))


def ewald_kernel(table_ref, filtered_ref, out_ref):
    bricks, atoms, _ = out_ref.shape
    for i in range(bricks):
        part = table_ref[i * atoms : (i + 1) * atoms, :]
        out_ref[i] = dot(part, filtered_ref[...]).astype(jnp.bfloat16)


def final_kernel(rows_ref, short_ref, e0_ref, e1_ref, e2_ref, e3_ref, wout_ref, out_ref):
    total = short_ref[...]
    for ref in (e0_ref, e1_ref, e2_ref, e3_ref):
        total = total + ref[...].astype(jnp.float32)
    moved = dot(total.astype(jnp.bfloat16), wout_ref[...])
    out_ref[...] = (rows_ref[...].astype(jnp.float32) + moved).astype(jnp.bfloat16)


def prepare_kernel(
    r0, r1, r2, low_ref, high_ref, p0, p1, p2, slots_ref, images_ref, win_ref, hidden, cols, pos, turned
):
    slots, atoms = slots_ref.shape
    weight = win_ref[...]
    own = (r0, r1, r2)
    for p in range(3):
        for q in range(3):
            brick = p * 3 + q
            if q == 1:
                rows, place = own[p][...], (p0, p1, p2)[p][...]
            else:
                ref = low_ref if q == 0 else high_ref
                rows = ref[p, 0:atoms, :]
                parts = ref[p, atoms:, :].astype(jnp.float32)
                place = (parts[0:3, :] + parts[8:11, :]) + parts[16:19, :]
            hidden[brick * atoms : (brick + 1) * atoms, :] = dot(rows, weight).astype(jnp.bfloat16)
            pos[0:3, brick * atoms : (brick + 1) * atoms] = place
    lane = 128
    for half in range(atoms // lane):
        cut = slice(half * lane, (half + 1) * lane)
        index = slots_ref[:, cut]
        image = images_ref[:, cut]
        place = index & (lane - 1)
        group = index >> 7
        near = [jnp.zeros((slots, lane), jnp.float32) for _ in range(3)]
        for r in range(9 * atoms // lane):
            here = group == r
            for c in range(3):
                table = jnp.broadcast_to(pos[c : c + 1, r * lane : (r + 1) * lane], (slots, lane))
                taken = jnp.take_along_axis(table, place, axis=1, mode="promise_in_bounds")
                near[c] = jnp.where(here, taken, near[c])
        first = (image >= 9).astype(jnp.int32) + (image >= 18).astype(jnp.int32)
        inside = image - 9 * first
        second = (inside >= 3).astype(jnp.int32) + (inside >= 6).astype(jnp.int32)
        third = inside - 3 * second
        square = jnp.zeros((slots, lane), jnp.float32)
        for c, offset in enumerate((first, second, third)):
            delta = near[c] + (offset - 1).astype(jnp.float32) * box_side - p1[c : c + 1, cut]
            square = square + delta * delta
        rest = jnp.sqrt(square + soft_sq) * ZOOM
        for k in range(3):
            rounded = rest.astype(jnp.bfloat16).astype(jnp.float32)
            turned[k * slots : (k + 1) * slots, cut] = rounded
            rest = rest - rounded
        turned[3 * slots : 4 * slots, cut] = ((lane + place) << group).astype(jnp.float32)
    cols[...] = turned[...].T.astype(jnp.bfloat16)


def short_kernel(first, count, scale, cols_ref, hidden, wrbf_ref, brbf_ref, wf_ref, sum_ref, out_ref, pairs, hot_a, hot_b):
    lane = 128
    atoms = cols_ref.shape[0]
    slots = cols_ref.shape[1] // 4
    basis_count, width = wrbf_ref.shape
    pairs[...] = jnp.zeros_like(pairs)
    pairs[0:basis_count, 0:width] = wrbf_ref[...]
    pairs[basis_count:, width:] = wrbf_ref[...]
    out_ref[...] = sum_ref[...]
    row = lax.broadcasted_iota(jnp.int32, (lane, 6 * lane), 0)
    column = lax.broadcasted_iota(jnp.int32, (lane, 6 * lane), 1)
    code_slot = jnp.where(row >= 3 * slots, row - 3 * slots - (column >> 7), -lane)
    dist_slot = jnp.where(row < 3 * slots, (row & (slots - 1)) - ((column - 4 * lane) >> 6), -lane)
    source = jnp.where(column < 4 * lane, code_slot, dist_slot)
    centers = (
        (lax.broadcasted_iota(jnp.int32, (1, lane), 1) & (basis_count - 1)).astype(jnp.float32)
        * (4.0 / (basis_count - 1))
        * ZOOM
    )
    lanes = lax.broadcasted_iota(jnp.int32, (16, lane), 1) + lane
    bias = brbf_ref[...] * math.log2(math.e)
    bias = jnp.concatenate([bias, bias], axis=1)
    groups = 9 * atoms // lane

    def spread(j):
        select = (source == 4 * j).astype(jnp.float32).astype(jnp.bfloat16)
        return dot(cols_ref[...], select)

    def make_hot(hot, wide):
        for i in range(4):
            code = wide[:, i * lane : (i + 1) * lane].astype(jnp.bfloat16)
            for g in range(groups):
                number = jnp.broadcast_to(
                    (lanes << g).astype(jnp.float32).astype(jnp.bfloat16)[None], (atoms // 16, 16, lane)
                ).reshape(atoms, lane)
                hot[i * atoms : (i + 1) * atoms, g * lane : (g + 1) * lane] = jnp.where(
                    code == number, jnp.bfloat16(1), jnp.bfloat16(0)
                )

    def filters_of(wide):
        inner = []
        for p in range(2):
            offset = wide[:, (4 + p) * lane : (5 + p) * lane] - centers
            basis = jnp.exp2(-(offset * offset)).astype(jnp.bfloat16)
            value = dot(basis, pairs[...]) * math.log2(math.e) + bias
            both = (jnp.log(1.0 + jnp.exp2(value)) - math.log(2.0)).astype(jnp.bfloat16)
            inner += [both[:, :width], both[:, width:]]
        return dot(jnp.concatenate(inner, axis=0), wf_ref[...])

    def add(filters, gathered):
        product = filters * gathered
        total = product[0:atoms]
        for i in range(1, 4):
            total = total + product[i * atoms : (i + 1) * atoms]
        out_ref[...] += total

    wide_first = spread(first)
    make_hot(hot_a, wide_first)

    def body(jj, carry):
        j = first + 2 * jj
        wide_b = spread(j + 1)
        make_hot(hot_b, wide_b)
        gathered_a = dot(hot_a[...], hidden[...])
        add(filters_of(spread(j)), gathered_a)
        wide_a = spread(j + 2)
        gathered_b = dot(hot_b[...], hidden[...])
        add(filters_of(wide_b), gathered_b)
        make_hot(hot_a, wide_a)
        return carry

    lax.fori_loop(0, count // 2, body, 0)
    out_ref[...] = out_ref[...] * scale


def local(
    features,
    positions,
    neighbours,
    images,
    wave,
    kgain,
    w_in,
    w_query,
    w_rbf,
    b_rbf,
    w_filter,
    w_out,
):
    f32, bf16 = jnp.float32, jnp.bfloat16
    rows = features[0, 0]
    place = positions[0, 0]
    atoms, width = rows.shape
    slots = neighbours.shape[2]
    roles = lax.axis_size("role")
    columns = lax.axis_size("atoms")
    atom_total = atoms * roles * columns
    waves = wave.shape[1]
    share = waves // roles
    piece = share // columns

    def from_role(block, shift):
        return lax.ppermute(block, "role", [((i + shift) % roles, i) for i in range(roles)])

    def from_column(block, shift):
        return lax.ppermute(
            block, "atoms", [((i + shift) % columns, i) for i in range(columns)]
        )

    shifts = (1, roles - 1, 2)
    place_of = {0: place, **{d: from_role(place, d) for d in shifts}}
    rows_of = {0: rows, **{d: from_role(rows, d) for d in shifts}}
    order = (0,) + shifts

    by_wave, by_atom = call(
        tables_kernel,
        [jax.ShapeDtypeStruct((2 * share, roles * atoms), bf16)]
        + [jax.ShapeDtypeStruct((roles * atoms, 2 * share), bf16)],
        [place_of[d] for d in order] + [wave],
        scratch=[pltpu.VMEM((3, roles * atoms), f32), pltpu.VMEM((share, 128), f32)],
        flops=40 * share * roles * atoms,
        nbytes=4 << 20,
        name="tables",
    )
    partial = call(
        functools.partial(structure_kernel, atom_total ** (-0.5)),
        jax.ShapeDtypeStruct((2 * share, width), bf16),
        [rows_of[d] for d in order] + [w_query, by_wave],
        scratch=[pltpu.VMEM((roles * atoms, width), bf16)],
        flops=2 * 2 * share * roles * atoms * width,
        nbytes=3 << 20,
        name="structure",
    )
    mine = lax.all_to_all(partial.reshape(columns, 2 * piece, width), "atoms", 0, 0)
    copies = call(
        reduce_kernel,
        jax.ShapeDtypeStruct((columns, 2 * piece, width), bf16),
        [mine, wave, kgain[None, :]],
        flops=2 * share * width,
        nbytes=1 << 20,
        name="reduce",
    )
    everyone = lax.all_to_all(copies, "atoms", 0, 0).reshape(2 * share, width)

    triple = (roles - 1, 0, 1)
    bundle = call(
        stack_kernel,
        jax.ShapeDtypeStruct((3, atoms + 32, width), bf16),
        [rows_of[d] for d in triple] + [place_of[d] for d in triple],
        scratch=[pltpu.VMEM((32, width), f32)],
        nbytes=1 << 20,
        name="stack",
    )
    low, high = from_column(bundle, columns - 1), from_column(bundle, 1)
    hidden, cols = call(
        prepare_kernel,
        [jax.ShapeDtypeStruct((9 * atoms, width), bf16), jax.ShapeDtypeStruct((atoms, 4 * slots), bf16)],
        [rows_of[d] for d in triple]
        + [low, high]
        + [place_of[d] for d in triple]
        + [neighbours[0, 0], images[0, 0], w_in],
        scratch=[pltpu.VMEM((8, 9 * atoms), f32), pltpu.VMEM((4 * slots, atoms), f32)],
        flops=2 * 9 * atoms * width * width,
        nbytes=4 << 20,
        name="prepare",
    )
    short = jnp.zeros((atoms, width), f32)
    quads = slots // 4
    for half in range(2):
        short = call(
            functools.partial(
                short_kernel, half * quads // 2, quads // 2, slots ** (-0.5) if half else 1.0
            ),
            jax.ShapeDtypeStruct((atoms, width), f32),
            [cols, hidden, w_rbf, b_rbf[None, :], w_filter, short],
            scratch=[
                pltpu.VMEM((128, 2 * width), bf16),
                pltpu.VMEM((4 * atoms, 9 * atoms), bf16),
                pltpu.VMEM((4 * atoms, 9 * atoms), bf16),
            ],
            flops=slots * atoms * 9 * atoms * width,
            nbytes=4 << 20,
            name="short%d" % half,
        )
    parts = call(
        ewald_kernel,
        jax.ShapeDtypeStruct((roles, atoms, width), bf16),
        [by_atom, everyone],
        flops=2 * 2 * share * roles * atoms * width,
        nbytes=4 << 20,
        name="ewald",
    )
    back = [parts[0]] + [from_role(parts[1 + i], roles - d) for i, d in enumerate(shifts)]
    result = call(
        final_kernel,
        jax.ShapeDtypeStruct((atoms, width), bf16),
        [rows, short] + back + [w_out],
        flops=2 * atoms * width * width,
        nbytes=1 << 20,
        name="final",
    )
    return result[None, None]


def solution(mesh):
    in_specs = (
        P("role", "atoms", None, None),
        P("role", "atoms", None, None),
        P("role", "atoms", None, None),
        P("role", "atoms", None, None),
        P(),
        P(),
        P(),
        P(),
        P(),
        P(),
        P(),
        P(),
    )
    out_specs = P("role", "atoms", None, None)
    return jax.shard_map(local, mesh=mesh, in_specs=in_specs, out_specs=out_specs, check_vma=False)
```

```python
import functools
import math

import jax
import jax.numpy as jnp
from jax import lax
from jax.experimental import pallas as pl
from jax.experimental.pallas import tpu as pltpu
from jax.sharding import PartitionSpec as P


box_side = 1.0
soft_sq = 0.01
damping = 64.0
ewald_scale = 0.25
SINE = (
    3.1415925800428712,
    -5.16770687881004,
    2.550031375353375,
    -0.5980451625033413,
    0.07722010591476362,
)
COSINE = (
    0.9999999534655706,
    -4.934792858503339,
    4.058411910098915,
    -1.331880131184001,
    0.21969673041819898,
)
ZOOM = 16.0 * math.sqrt(math.log2(math.e))
VMEM = pl.BlockSpec(memory_space=pltpu.VMEM)


def call(body, out, ins, scratch=(), flops=0, nbytes=0, trans=0, grant=16):
    multiple = isinstance(out, (list, tuple))
    return pl.pallas_call(
        body,
        out_shape=out,
        in_specs=[VMEM] * len(ins),
        out_specs=[VMEM] * len(out) if multiple else VMEM,
        scratch_shapes=list(scratch),
        compiler_params=pltpu.CompilerParams(vmem_limit_bytes=grant << 20),
        cost_estimate=pl.CostEstimate(flops=flops, bytes_accessed=nbytes, transcendentals=trans),
    )(*ins)


def dot(left, right):
    return jnp.dot(left, right, preferred_element_type=jnp.float32)


def sine_cosine(turns):
    rest = turns - jnp.round(turns)
    square = rest * rest
    odd = SINE[-1]
    for coef in SINE[-2::-1]:
        odd = odd * square + coef
    even = COSINE[-1]
    for coef in COSINE[-2::-1]:
        even = even * square + coef
    half = odd * rest
    return 2.0 * (half * even), 1.0 - 2.0 * (half * half)


def begin_kernel(wave_ref, rows_ref, wq_ref, cols, rows_out, wq_out):
    share = cols.shape[0]
    role = lax.axis_index("role")
    for i in range(share // 128):
        first = pl.multiple_of(role * share + i * 128, 128)
        cols[i * 128 : (i + 1) * 128, 0:3] = wave_ref[:, pl.ds(first, 128)].astype(jnp.float32).T
    rows_out[...] = rows_ref[...]
    wq_out[...] = wq_ref[...]


def tables_kernel(*refs):
    pos_refs, (cols, by_wave, by_atom, pos) = refs[:4], refs[4:]
    atoms = pos_refs[0].shape[1]
    for i, ref in enumerate(pos_refs):
        pos[:, i * atoms : (i + 1) * atoms] = ref[...]
    share = by_wave.shape[0] // 2
    step = 64
    total = pos.shape[1]

    def block(j, carry):
        waves = cols[pl.ds(pl.multiple_of(j * step, step), step), :]
        turns = (
            waves[:, 0:1] * pos[0:1, :] + waves[:, 1:2] * pos[1:2, :] + waves[:, 2:3] * pos[2:3, :]
        )
        sine, cosine = sine_cosine(turns)
        both = jnp.stack(
            [cosine.reshape(step // 8, 8, total), sine.reshape(step // 8, 8, total)], axis=1
        ).reshape(2 * step, total)
        part = pl.ds(pl.multiple_of(j * 2 * step, 2 * step), 2 * step)
        by_wave[part, :] = both.astype(jnp.bfloat16)
        by_atom[:, part] = both.T.astype(jnp.bfloat16)
        return carry

    lax.fori_loop(0, share // step, block, 0)


def structure_kernel(scale, *refs):
    rows_refs, (wq_ref, table, out_ref, queries) = refs[:4], refs[4:]
    atoms = rows_refs[0].shape[0]
    weight = wq_ref[...]
    for i, rows in enumerate(rows_refs):
        queries[i * atoms : (i + 1) * atoms, :] = dot(rows[...], weight).astype(jnp.bfloat16)
    out_ref[...] = (dot(table[...], queries[...]) * scale).astype(jnp.bfloat16)


def stack_kernel(*refs):
    rows_refs, pos_refs, (out_ref, parts) = refs[:3], refs[3:6], refs[6:]
    atoms = rows_refs[0].shape[0]
    parts[...] = jnp.zeros_like(parts)
    for i in range(3):
        out_ref[i, 0:atoms, :] = rows_refs[i][...]
        rest = pos_refs[i][...]
        for k in range(3):
            rounded = rest.astype(jnp.bfloat16).astype(jnp.float32)
            parts[8 * k : 8 * k + 3, :] = rounded
            rest = rest - rounded
        out_ref[i, atoms:, :] = parts[...].astype(jnp.bfloat16)


def reduce_kernel(mine_ref, wave_ref, kgain_ref, out_ref):
    columns, rows, width = mine_ref.shape
    piece = rows // 2
    share = columns * piece
    first = lax.axis_index("role") * share + lax.axis_index("atoms") * piece
    start = pl.multiple_of((first // 128) * 128, 128)
    waves = wave_ref[:, pl.ds(start, 128)].astype(jnp.float32)
    squares = jnp.broadcast_to(jnp.sum(waves * waves, axis=0, keepdims=True), (piece, 128))
    lanes = lax.broadcasted_iota(jnp.int32, (piece, 128), 1)
    wanted = lax.broadcasted_iota(jnp.int32, (piece, 128), 0) + (first - start)
    square = jnp.sum(jnp.where(lanes == wanted, squares, 0.0), axis=1, keepdims=True)
    k_filter = ewald_scale * kgain_ref[...] * (jnp.exp(-square / damping) / square)
    total = jnp.sum(mine_ref[...].astype(jnp.float32), axis=0)
    filtered = total * jnp.concatenate([k_filter, k_filter], axis=0)
    out_ref[...] = jnp.broadcast_to(filtered.astype(jnp.bfloat16)[None], (columns, rows, width))


def ewald_kernel(table_ref, filtered_ref, out_ref):
    bricks, atoms, _ = out_ref.shape
    for i in range(bricks):
        part = table_ref[i * atoms : (i + 1) * atoms, :]
        out_ref[i] = dot(part, filtered_ref[...]).astype(jnp.bfloat16)


def final_kernel(rows_ref, short_ref, e0_ref, e1_ref, e2_ref, e3_ref, wout_ref, out_ref):
    total = short_ref[...]
    for ref in (e0_ref, e1_ref, e2_ref, e3_ref):
        total = total + ref[...].astype(jnp.float32)
    moved = dot(total.astype(jnp.bfloat16), wout_ref[...])
    out_ref[...] = (rows_ref[...].astype(jnp.float32) + moved).astype(jnp.bfloat16)


def prepare_kernel(
    r0, r1, r2, low_ref, high_ref, p0, p1, p2, slots_ref, images_ref, win_ref, hidden, cols, pos, turned
):
    slots, atoms = slots_ref.shape
    weight = win_ref[...]
    own = (r0, r1, r2)
    for p in range(3):
        for q in range(3):
            brick = p * 3 + q
            if q == 1:
                rows, place = own[p][...], (p0, p1, p2)[p][...]
            else:
                ref = low_ref if q == 0 else high_ref
                rows = ref[p, 0:atoms, :]
                parts = ref[p, atoms:, :].astype(jnp.float32)
                place = (parts[0:3, :] + parts[8:11, :]) + parts[16:19, :]
            hidden[brick * atoms : (brick + 1) * atoms, :] = dot(rows, weight).astype(jnp.bfloat16)
            pos[0:3, brick * atoms : (brick + 1) * atoms] = place
    lane = 128
    for half in range(atoms // lane):
        cut = slice(half * lane, (half + 1) * lane)
        index = slots_ref[:, cut]
        image = images_ref[:, cut]
        place = index & (lane - 1)
        group = index >> 7
        near = [jnp.zeros((slots, lane), jnp.float32) for _ in range(3)]
        for r in range(9 * atoms // lane):
            here = group == r
            for c in range(3):
                table = jnp.broadcast_to(pos[c : c + 1, r * lane : (r + 1) * lane], (slots, lane))
                taken = jnp.take_along_axis(table, place, axis=1, mode="promise_in_bounds")
                near[c] = jnp.where(here, taken, near[c])
        first = (image >= 9).astype(jnp.int32) + (image >= 18).astype(jnp.int32)
        inside = image - 9 * first
        second = (inside >= 3).astype(jnp.int32) + (inside >= 6).astype(jnp.int32)
        third = inside - 3 * second
        square = jnp.zeros((slots, lane), jnp.float32)
        for c, offset in enumerate((first, second, third)):
            delta = near[c] + (offset - 1).astype(jnp.float32) * box_side - p1[c : c + 1, cut]
            square = square + delta * delta
        rest = jnp.sqrt(square + soft_sq) * ZOOM
        for k in range(3):
            rounded = rest.astype(jnp.bfloat16).astype(jnp.float32)
            turned[k * slots : (k + 1) * slots, cut] = rounded
            rest = rest - rounded
        turned[3 * slots : 4 * slots, cut] = ((lane + place) << group).astype(jnp.float32)
    cols[...] = turned[...].T.astype(jnp.bfloat16)


def short_kernel(first, count, scale, cols_ref, hidden, wrbf_ref, brbf_ref, wf_ref, sum_ref, out_ref, pairs):
    lane = 128
    atoms = cols_ref.shape[0]
    slots = cols_ref.shape[1] // 4
    basis_count, width = wrbf_ref.shape
    pairs[...] = jnp.zeros_like(pairs)
    pairs[0:basis_count, 0:width] = wrbf_ref[...]
    pairs[basis_count:, width:] = wrbf_ref[...]
    out_ref[...] = sum_ref[...]
    row = lax.broadcasted_iota(jnp.int32, (lane, 6 * lane), 0)
    column = lax.broadcasted_iota(jnp.int32, (lane, 6 * lane), 1)
    code_slot = jnp.where(row >= 3 * slots, row - 3 * slots - (column >> 7), -lane)
    dist_slot = jnp.where(row < 3 * slots, (row & (slots - 1)) - ((column - 4 * lane) >> 6), -lane)
    source = jnp.where(column < 4 * lane, code_slot, dist_slot)
    centers = (
        (lax.broadcasted_iota(jnp.int32, (1, lane), 1) & (basis_count - 1)).astype(jnp.float32)
        * (4.0 / (basis_count - 1))
        * ZOOM
    )
    lanes = lax.broadcasted_iota(jnp.int32, (16, lane), 1) + lane
    bias = brbf_ref[...] * math.log2(math.e)
    bias = jnp.concatenate([bias, bias], axis=1)
    groups = 9 * atoms // lane

    def spread(j):
        select = (source == 4 * j).astype(jnp.float32).astype(jnp.bfloat16)
        return dot(cols_ref[...], select)

    def hot_of(wide):
        codes = [
            wide[:, i * lane : (i + 1) * lane].astype(jnp.bfloat16) for i in range(4)
        ]
        code = jnp.concatenate(codes, axis=0)
        parts = []
        for g in range(groups):
            number = jnp.broadcast_to(
                (lanes << g).astype(jnp.float32).astype(jnp.bfloat16)[None],
                (4 * atoms // 16, 16, lane),
            ).reshape(4 * atoms, lane)
            parts.append(jnp.where(code == number, jnp.bfloat16(1), jnp.bfloat16(0)))
        return jnp.concatenate(parts, axis=1)

    def filters_of(wide):
        inner = []
        for p in range(2):
            offset = wide[:, (4 + p) * lane : (5 + p) * lane] - centers
            basis = jnp.exp2(-(offset * offset)).astype(jnp.bfloat16)
            value = dot(basis, pairs[...]) * math.log2(math.e) + bias
            both = (jnp.log(1.0 + jnp.exp2(value)) - math.log(2.0)).astype(jnp.bfloat16)
            inner += [both[:, :width], both[:, width:]]
        return dot(jnp.concatenate(inner, axis=0), wf_ref[...])

    def add(filters, gathered):
        product = filters * gathered
        total = product[0:atoms]
        for i in range(1, 4):
            total = total + product[i * atoms : (i + 1) * atoms]
        out_ref[...] += total

    def body(j, carry):
        wide = spread(first + j)
        gathered = dot(hot_of(wide), hidden[...])
        add(filters_of(wide), gathered)
        return carry

    lax.fori_loop(0, count, body, 0)
    out_ref[...] = out_ref[...] * scale


def block(
    features,
    positions,
    neighbours,
    images,
    wave,
    kgain,
    w_in,
    w_query,
    w_rbf,
    b_rbf,
    w_filter,
    w_out,
):
    f32, bf16 = jnp.float32, jnp.bfloat16
    rows = features[0, 0]
    place = positions[0, 0]
    atoms, width = rows.shape
    slots = neighbours.shape[2]
    roles = lax.axis_size("role")
    columns = lax.axis_size("atoms")
    atom_total = atoms * roles * columns
    waves = wave.shape[1]
    share = waves // roles
    piece = share // columns

    def from_role(block, shift):
        return lax.ppermute(block, "role", [((i + shift) % roles, i) for i in range(roles)])

    def from_column(block, shift):
        return lax.ppermute(
            block, "atoms", [((i + shift) % columns, i) for i in range(columns)]
        )

    shifts = (1, roles - 1, 2)
    place_of = {0: place, **{d: from_role(place, d) for d in shifts}}
    rows_of = {0: rows, **{d: from_role(rows, d) for d in shifts}}
    wave_cols, near_own, near_query = call(
        begin_kernel,
        [
            jax.ShapeDtypeStruct((share, 128), f32),
            jax.ShapeDtypeStruct((atoms, width), bf16),
            jax.ShapeDtypeStruct((width, width), bf16),
        ],
        [wave, rows, w_query],
        nbytes=1 << 19,
    )
    order = (0,) + shifts

    by_wave, by_atom = call(
        tables_kernel,
        [jax.ShapeDtypeStruct((2 * share, roles * atoms), bf16)]
        + [jax.ShapeDtypeStruct((roles * atoms, 2 * share), bf16)],
        [place_of[d] for d in order] + [wave_cols],
        scratch=[pltpu.VMEM((3, roles * atoms), f32)],
        flops=40 * share * roles * atoms,
        nbytes=4 << 20,
    )
    partial = call(
        functools.partial(structure_kernel, atom_total ** (-0.5)),
        jax.ShapeDtypeStruct((2 * share, width), bf16),
        [near_own] + [rows_of[d] for d in shifts] + [near_query, by_wave],
        scratch=[pltpu.VMEM((roles * atoms, width), bf16)],
        flops=2 * 2 * share * roles * atoms * width,
        nbytes=3 << 20,
    )
    mine = lax.all_to_all(partial.reshape(columns, 2 * piece, width), "atoms", 0, 0)
    copies = call(
        reduce_kernel,
        jax.ShapeDtypeStruct((columns, 2 * piece, width), bf16),
        [mine, wave, kgain[None, :]],
        flops=2 * share * width,
        nbytes=1 << 20,
    )
    everyone = lax.all_to_all(copies, "atoms", 0, 0).reshape(2 * share, width)

    triple = (roles - 1, 0, 1)
    bundle = call(
        stack_kernel,
        jax.ShapeDtypeStruct((3, atoms + 32, width), bf16),
        [rows_of[roles - 1], near_own, rows_of[1]] + [place_of[d] for d in triple],
        scratch=[pltpu.VMEM((32, width), f32)],
        nbytes=1 << 20,
    )
    low, high = from_column(bundle, columns - 1), from_column(bundle, 1)
    hidden, cols = call(
        prepare_kernel,
        [jax.ShapeDtypeStruct((9 * atoms, width), bf16), jax.ShapeDtypeStruct((atoms, 4 * slots), bf16)],
        [rows_of[roles - 1], near_own, rows_of[1]]
        + [low, high]
        + [place_of[d] for d in triple]
        + [neighbours[0, 0], images[0, 0], w_in],
        scratch=[pltpu.VMEM((8, 9 * atoms), f32), pltpu.VMEM((4 * slots, atoms), f32)],
        flops=2 * 9 * atoms * width * width,
        nbytes=4 << 20,
    )
    short = jnp.zeros((atoms, width), f32)
    quads = slots // 4
    for half in range(2):
        short = call(
            functools.partial(
                short_kernel, half * quads // 2, quads // 2, slots ** (-0.5) if half else 1.0
            ),
            jax.ShapeDtypeStruct((atoms, width), f32),
            [cols, hidden, w_rbf, b_rbf[None, :], w_filter, short],
            scratch=[pltpu.VMEM((128, 2 * width), bf16)],
            grant=32,
            flops=slots * atoms * 9 * atoms * width,
            nbytes=4 << 20,
        )
    parts = call(
        ewald_kernel,
        jax.ShapeDtypeStruct((roles, atoms, width), bf16),
        [by_atom, everyone],
        flops=2 * 2 * share * roles * atoms * width,
        nbytes=4 << 20,
    )
    back = [parts[0]] + [from_role(parts[1 + i], roles - d) for i, d in enumerate(shifts)]
    result = call(
        final_kernel,
        jax.ShapeDtypeStruct((atoms, width), bf16),
        [rows, short] + back + [w_out],
        flops=2 * atoms * width * width,
        nbytes=1 << 20,
    )
    return result[None, None]


def solution(mesh):
    in_specs = (
        P("role", "atoms", None, None),
        P("role", "atoms", None, None),
        P("role", "atoms", None, None),
        P("role", "atoms", None, None),
        P(),
        P(),
        P(),
        P(),
        P(),
        P(),
        P(),
        P(),
    )
    out_specs = P("role", "atoms", None, None)
    return jax.shard_map(block, mesh=mesh, in_specs=in_specs, out_specs=out_specs, check_vma=False)
```

```python
import functools
import math

import jax
import jax.numpy as jnp
from jax import lax
from jax.experimental import pallas as pl
from jax.experimental.pallas import tpu as pltpu
from jax.sharding import PartitionSpec as P


box_side = 1.0
soft_sq = 0.01
damping = 64.0
ewald_scale = 0.25
SINE = (
    3.1415925800428712,
    -5.16770687881004,
    2.550031375353375,
    -0.5980451625033413,
    0.07722010591476362,
)
COSINE = (
    0.9999999534655706,
    -4.934792858503339,
    4.058411910098915,
    -1.331880131184001,
    0.21969673041819898,
)
ZOOM = 16.0 * math.sqrt(math.log2(math.e))
VMEM = pl.BlockSpec(memory_space=pltpu.VMEM)


def call(body, out, ins, scratch=(), flops=0, nbytes=0, trans=0, grant=16):
    multiple = isinstance(out, (list, tuple))
    return pl.pallas_call(
        body,
        out_shape=out,
        in_specs=[VMEM] * len(ins),
        out_specs=[VMEM] * len(out) if multiple else VMEM,
        scratch_shapes=list(scratch),
        compiler_params=pltpu.CompilerParams(vmem_limit_bytes=grant << 20),
        cost_estimate=pl.CostEstimate(flops=flops, bytes_accessed=nbytes, transcendentals=trans),
    )(*ins)


def dot(left, right):
    return jnp.dot(left, right, preferred_element_type=jnp.float32)


def sine_cosine(turns):
    rest = turns - jnp.round(turns)
    square = rest * rest
    odd = SINE[-1]
    for coef in SINE[-2::-1]:
        odd = odd * square + coef
    even = COSINE[-1]
    for coef in COSINE[-2::-1]:
        even = even * square + coef
    half = odd * rest
    return 2.0 * (half * even), 1.0 - 2.0 * (half * half)


def begin_kernel(wave_ref, rows_ref, place_ref, wq_ref, cols, rows_out, place_out, wq_out, flat):
    share = cols.shape[0]
    role = lax.axis_index("role")
    flat[...] = jnp.zeros_like(flat)
    for i in range(share // 128):
        first = pl.multiple_of(role * share + i * 128, 128)
        waves = wave_ref[:, pl.ds(first, 128)].astype(jnp.float32)
        for k in range(3):
            flat[3 * k : 3 * k + 3, :] = waves
        cols[i * 128 : (i + 1) * 128, :] = flat[...].T.astype(jnp.bfloat16)
    rows_out[...] = rows_ref[...]
    place_out[...] = place_ref[...]
    wq_out[...] = wq_ref[...]


def tables_kernel(*refs):
    pos_refs, (cols, by_wave, by_atom, pos, parts) = refs[:4], refs[4:]
    atoms = pos_refs[0].shape[1]
    total = pos.shape[1]
    pos[...] = jnp.zeros_like(pos)
    for i, ref in enumerate(pos_refs):
        rest = ref[...]
        for k in range(3):
            rounded = rest.astype(jnp.bfloat16).astype(jnp.float32)
            pos[3 * k : 3 * k + 3, i * atoms : (i + 1) * atoms] = rounded
            rest = rest - rounded
    parts[...] = pos[...].astype(jnp.bfloat16)
    share = by_wave.shape[0] // 2
    step = 64

    def block(j, carry):
        waves = cols[pl.ds(pl.multiple_of(j * step, step), step), :]
        sine, cosine = sine_cosine(dot(waves, parts[...]))
        both = jnp.stack(
            [cosine.reshape(step // 8, 8, total), sine.reshape(step // 8, 8, total)], axis=1
        ).reshape(2 * step, total)
        part = pl.ds(pl.multiple_of(j * 2 * step, 2 * step), 2 * step)
        by_wave[part, :] = both.astype(jnp.bfloat16)
        by_atom[:, part] = both.T.astype(jnp.bfloat16)
        return carry

    lax.fori_loop(0, share // step, block, 0)


def core_half(size, other):
    core = lax.axis_index("atoms") & 1
    core = 1 - core if other else core
    return pl.ds(pl.multiple_of(core * size, size), size)


def send_kernel(scale, *refs):
    rows_refs, (wq_ref, table, out_ref, queries) = refs[:4], refs[4:]
    atoms = rows_refs[0].shape[0]
    weight = wq_ref[...]
    for i, rows in enumerate(rows_refs):
        queries[i * atoms : (i + 1) * atoms, :] = dot(rows[...], weight).astype(jnp.bfloat16)
    part = core_half(out_ref.shape[0], True)
    out_ref[...] = (dot(table[part, :], queries[...]) * scale).astype(jnp.bfloat16)


def keep_kernel(scale, queries, table, got_ref, out_ref):
    part = core_half(out_ref.shape[0], False)
    own = dot(table[part, :], queries[...]) * scale
    out_ref[...] = (own + got_ref[...].astype(jnp.float32)).astype(jnp.bfloat16)


def stack_kernel(*refs):
    rows_refs, pos_refs, (out_ref, parts) = refs[:3], refs[3:6], refs[6:]
    atoms = rows_refs[0].shape[0]
    parts[...] = jnp.zeros_like(parts)
    for i in range(3):
        out_ref[i, 0:atoms, :] = rows_refs[i][...]
        rest = pos_refs[i][...]
        for k in range(3):
            rounded = rest.astype(jnp.bfloat16).astype(jnp.float32)
            parts[8 * k : 8 * k + 3, :] = rounded
            rest = rest - rounded
        out_ref[i, atoms:, :] = parts[...].astype(jnp.bfloat16)


def reduce_kernel(mine_ref, wave_ref, kgain_ref, out_ref):
    chips, rows, width = mine_ref.shape
    piece = rows // 2
    share = 2 * chips * piece
    column = lax.axis_index("atoms")
    first = lax.axis_index("role") * share + ((column & 1) * chips + (column >> 1)) * piece
    start = pl.multiple_of((first // 128) * 128, 128)
    waves = wave_ref[:, pl.ds(start, 128)].astype(jnp.float32)
    squares = jnp.broadcast_to(jnp.sum(waves * waves, axis=0, keepdims=True), (piece, 128))
    lanes = lax.broadcasted_iota(jnp.int32, (piece, 128), 1)
    wanted = lax.broadcasted_iota(jnp.int32, (piece, 128), 0) + (first - start)
    square = jnp.sum(jnp.where(lanes == wanted, squares, 0.0), axis=1, keepdims=True)
    k_filter = ewald_scale * kgain_ref[...] * (jnp.exp(-square / damping) / square)
    total = jnp.sum(mine_ref[...].astype(jnp.float32), axis=0)
    filtered = total * jnp.concatenate([k_filter, k_filter], axis=0)
    out_ref[...] = jnp.broadcast_to(filtered.astype(jnp.bfloat16)[None], (chips, rows, width))


def ewald_kernel(table_ref, own_ref, other_ref, *out_refs):
    atoms, _ = out_refs[0].shape
    size = own_ref.shape[0]
    for i, out_ref in enumerate(out_refs):
        part = slice(i * atoms, (i + 1) * atoms)
        total = dot(table_ref[part, core_half(size, False)], own_ref[...])
        total = total + dot(table_ref[part, core_half(size, True)], other_ref[...])
        out_ref[...] = total.astype(jnp.bfloat16)


def final_kernel(rows_ref, short_ref, e0_ref, e1_ref, e2_ref, e3_ref, wout_ref, out_ref):
    total = short_ref[...]
    for ref in (e0_ref, e1_ref, e2_ref, e3_ref):
        total = total + ref[...].astype(jnp.float32)
    moved = dot(total.astype(jnp.bfloat16), wout_ref[...])
    out_ref[...] = (rows_ref[...].astype(jnp.float32) + moved).astype(jnp.bfloat16)


def prepare_kernel(
    r0, r1, r2, low_ref, high_ref, p0, p1, p2, slots_ref, images_ref, win_ref, hidden, cols, pos, turned
):
    slots, atoms = slots_ref.shape
    weight = win_ref[...]
    own = (r0, r1, r2)
    for p in range(3):
        for q in range(3):
            brick = p * 3 + q
            if q == 1:
                rows, place = own[p][...], (p0, p1, p2)[p][...]
            else:
                ref = low_ref if q == 0 else high_ref
                rows = ref[p, 0:atoms, :]
                parts = ref[p, atoms:, :].astype(jnp.float32)
                place = (parts[0:3, :] + parts[8:11, :]) + parts[16:19, :]
            hidden[brick * atoms : (brick + 1) * atoms, :] = dot(rows, weight).astype(jnp.bfloat16)
            pos[0:3, brick * atoms : (brick + 1) * atoms] = place
    lane = 128
    for half in range(atoms // lane):
        cut = slice(half * lane, (half + 1) * lane)
        index = slots_ref[:, cut]
        image = images_ref[:, cut]
        place = index & (lane - 1)
        group = index >> 7
        near = [jnp.zeros((slots, lane), jnp.float32) for _ in range(3)]
        for r in range(9 * atoms // lane):
            here = group == r
            for c in range(3):
                table = jnp.broadcast_to(pos[c : c + 1, r * lane : (r + 1) * lane], (slots, lane))
                taken = jnp.take_along_axis(table, place, axis=1, mode="promise_in_bounds")
                near[c] = jnp.where(here, taken, near[c])
        first = (image >= 9).astype(jnp.int32) + (image >= 18).astype(jnp.int32)
        inside = image - 9 * first
        second = (inside >= 3).astype(jnp.int32) + (inside >= 6).astype(jnp.int32)
        third = inside - 3 * second
        square = jnp.zeros((slots, lane), jnp.float32)
        for c, offset in enumerate((first, second, third)):
            delta = near[c] + (offset - 1).astype(jnp.float32) * box_side - p1[c : c + 1, cut]
            square = square + delta * delta
        rest = jnp.sqrt(square + soft_sq) * ZOOM
        for k in range(3):
            rounded = rest.astype(jnp.bfloat16).astype(jnp.float32)
            turned[k * slots : (k + 1) * slots, cut] = rounded
            rest = rest - rounded
        turned[3 * slots : 4 * slots, cut] = ((lane + place) << group).astype(jnp.float32)
    cols[...] = turned[...].T.astype(jnp.bfloat16)


def short_kernel(first, count, scale, cols_ref, hidden, wrbf_ref, brbf_ref, wf_ref, sum_ref, out_ref, pairs):
    lane = 128
    atoms = cols_ref.shape[0]
    slots = cols_ref.shape[1] // 4
    basis_count, width = wrbf_ref.shape
    pairs[...] = jnp.zeros_like(pairs)
    pairs[0:basis_count, 0:width] = wrbf_ref[...]
    pairs[basis_count:, width:] = wrbf_ref[...]
    out_ref[...] = sum_ref[...]
    row = lax.broadcasted_iota(jnp.int32, (lane, 6 * lane), 0)
    column = lax.broadcasted_iota(jnp.int32, (lane, 6 * lane), 1)
    code_slot = jnp.where(row >= 3 * slots, row - 3 * slots - (column >> 7), -lane)
    dist_slot = jnp.where(row < 3 * slots, (row & (slots - 1)) - ((column - 4 * lane) >> 6), -lane)
    source = jnp.where(column < 4 * lane, code_slot, dist_slot)
    centers = (
        (lax.broadcasted_iota(jnp.int32, (1, lane), 1) & (basis_count - 1)).astype(jnp.float32)
        * (4.0 / (basis_count - 1))
        * ZOOM
    )
    lanes = lax.broadcasted_iota(jnp.int32, (16, lane), 1) + lane
    bias = brbf_ref[...] * math.log2(math.e)
    bias = jnp.concatenate([bias, bias], axis=1)
    groups = 9 * atoms // lane

    def spread(j):
        select = (source == 4 * j).astype(jnp.float32).astype(jnp.bfloat16)
        return dot(cols_ref[...], select)

    def hot_of(wide):
        codes = [
            wide[:, i * lane : (i + 1) * lane].astype(jnp.bfloat16) for i in range(4)
        ]
        code = jnp.concatenate(codes, axis=0)
        parts = []
        for g in range(groups):
            number = jnp.broadcast_to(
                (lanes << g).astype(jnp.float32).astype(jnp.bfloat16)[None],
                (4 * atoms // 16, 16, lane),
            ).reshape(4 * atoms, lane)
            parts.append(jnp.where(code == number, jnp.bfloat16(1), jnp.bfloat16(0)))
        return jnp.concatenate(parts, axis=1)

    def filters_of(wide):
        inner = []
        for p in range(2):
            offset = wide[:, (4 + p) * lane : (5 + p) * lane] - centers
            basis = jnp.exp2(-(offset * offset)).astype(jnp.bfloat16)
            value = dot(basis, pairs[...]) * math.log2(math.e) + bias
            both = (jnp.log(1.0 + jnp.exp2(value)) - math.log(2.0)).astype(jnp.bfloat16)
            inner += [both[:, :width], both[:, width:]]
        return dot(jnp.concatenate(inner, axis=0), wf_ref[...])

    def add(filters, gathered):
        product = filters * gathered
        total = product[0:atoms]
        for i in range(1, 4):
            total = total + product[i * atoms : (i + 1) * atoms]
        out_ref[...] += total

    def body(j, carry):
        wide = spread(first + j)
        gathered = dot(hot_of(wide), hidden[...])
        add(filters_of(wide), gathered)
        return carry

    lax.fori_loop(0, count, body, 0)
    out_ref[...] = out_ref[...] * scale


def block(
    features,
    positions,
    neighbours,
    images,
    wave,
    kgain,
    w_in,
    w_query,
    w_rbf,
    b_rbf,
    w_filter,
    w_out,
):
    f32, bf16 = jnp.float32, jnp.bfloat16
    rows = features[0, 0]
    place = positions[0, 0]
    atoms, width = rows.shape
    slots = neighbours.shape[2]
    roles = lax.axis_size("role")
    columns = lax.axis_size("atoms")
    atom_total = atoms * roles * columns
    waves = wave.shape[1]
    share = waves // roles
    piece = share // columns

    def from_role(block, shift):
        return lax.ppermute(block, "role", [((i + shift) % roles, i) for i in range(roles)])

    def from_column(block, shift):
        return lax.ppermute(
            block, "atoms", [((i + shift) % columns, i) for i in range(columns)]
        )

    shifts = (1, roles - 1, 2)
    order = (0,) + shifts
    wave_cols, rows, place, near_query = call(
        begin_kernel,
        [
            jax.ShapeDtypeStruct((share, 128), bf16),
            jax.ShapeDtypeStruct((atoms, width), bf16),
            jax.ShapeDtypeStruct((3, atoms), f32),
            jax.ShapeDtypeStruct((width, width), bf16),
        ],
        [wave, rows, place, w_query],
        scratch=[pltpu.VMEM((128, 128), f32)],
        nbytes=1 << 19,
    )
    place_of = {0: place, **{d: from_role(place, d) for d in shifts}}
    rows_of = {0: rows, **{d: from_role(rows, d) for d in shifts}}
    by_wave, by_atom = call(
        tables_kernel,
        [jax.ShapeDtypeStruct((2 * share, roles * atoms), bf16)]
        + [jax.ShapeDtypeStruct((roles * atoms, 2 * share), bf16)],
        [place_of[d] for d in order] + [wave_cols],
        scratch=[pltpu.VMEM((128, roles * atoms), f32), pltpu.VMEM((128, roles * atoms), bf16)],
        flops=40 * share * roles * atoms,
        nbytes=4 << 20,
    )
    norm = atom_total ** (-0.5)
    partner = [(i, i ^ 1) for i in range(columns)]
    same_core = [list(range(c, columns, 2)) for c in range(2)]
    sent, queries = call(
        functools.partial(send_kernel, norm),
        [jax.ShapeDtypeStruct((share, width), bf16), jax.ShapeDtypeStruct((roles * atoms, width), bf16)],
        [rows_of[d] for d in order] + [near_query, by_wave],
        flops=2 * share * roles * atoms * width,
        nbytes=3 << 20,
    )
    got = lax.ppermute(sent, "atoms", partner)
    kept = call(
        functools.partial(keep_kernel, norm),
        jax.ShapeDtypeStruct((share, width), bf16),
        [queries, by_wave, got],
        flops=2 * share * roles * atoms * width,
        nbytes=2 << 20,
    )
    chunks = (columns // 2, 2 * piece, width)
    mine = lax.all_to_all(kept.reshape(chunks), "atoms", 0, 0, axis_index_groups=same_core)
    copies = call(
        reduce_kernel,
        jax.ShapeDtypeStruct(chunks, bf16),
        [mine, wave, kgain[None, :]],
        flops=2 * share * width,
        nbytes=1 << 20,
    )
    half_own = lax.all_to_all(copies, "atoms", 0, 0, axis_index_groups=same_core).reshape(
        share, width
    )
    half_other = lax.ppermute(half_own, "atoms", partner)

    triple = (roles - 1, 0, 1)
    bundle = call(
        stack_kernel,
        jax.ShapeDtypeStruct((3, atoms + 32, width), bf16),
        [rows_of[d] for d in triple] + [place_of[d] for d in triple],
        scratch=[pltpu.VMEM((32, width), f32)],
        nbytes=1 << 20,
    )
    low, high = from_column(bundle, columns - 1), from_column(bundle, 1)
    hidden, cols = call(
        prepare_kernel,
        [jax.ShapeDtypeStruct((9 * atoms, width), bf16), jax.ShapeDtypeStruct((atoms, 4 * slots), bf16)],
        [rows_of[d] for d in triple]
        + [low, high]
        + [place_of[d] for d in triple]
        + [neighbours[0, 0], images[0, 0], w_in],
        scratch=[pltpu.VMEM((8, 9 * atoms), f32), pltpu.VMEM((4 * slots, atoms), f32)],
        flops=2 * 9 * atoms * width * width,
        nbytes=4 << 20,
    )
    short = jnp.zeros((atoms, width), f32)
    quads = slots // 4
    for half in range(2):
        short = call(
            functools.partial(
                short_kernel, half * quads // 2, quads // 2, slots ** (-0.5) if half else 1.0
            ),
            jax.ShapeDtypeStruct((atoms, width), f32),
            [cols, hidden, w_rbf, b_rbf[None, :], w_filter, short],
            scratch=[pltpu.VMEM((128, 2 * width), bf16)],
            grant=32,
            flops=slots * atoms * 9 * atoms * width,
            nbytes=4 << 20,
        )
    parts = call(
        ewald_kernel,
        [jax.ShapeDtypeStruct((atoms, width), bf16)] * roles,
        [by_atom, half_own, half_other],
        flops=2 * 2 * share * roles * atoms * width,
        nbytes=4 << 20,
    )
    back = [parts[0]] + [from_role(parts[1 + i], roles - d) for i, d in enumerate(shifts)]
    result = call(
        final_kernel,
        jax.ShapeDtypeStruct((atoms, width), bf16),
        [rows, short] + back + [w_out],
        flops=2 * atoms * width * width,
        nbytes=1 << 20,
    )
    return result[None, None]


def solution(mesh):
    in_specs = (
        P("role", "atoms", None, None),
        P("role", "atoms", None, None),
        P("role", "atoms", None, None),
        P("role", "atoms", None, None),
        P(),
        P(),
        P(),
        P(),
        P(),
        P(),
        P(),
        P(),
    )
    out_specs = P("role", "atoms", None, None)
    return jax.shard_map(block, mesh=mesh, in_specs=in_specs, out_specs=out_specs, check_vma=False)
```

```python
import functools
import math

import jax
import jax.numpy as jnp
from jax import lax
from jax.experimental import pallas as pl
from jax.experimental.pallas import tpu as pltpu
from jax.sharding import PartitionSpec as P


box_side = 1.0
soft_sq = 0.01
damping = 64.0
ewald_scale = 0.25
SINE = (
    3.1415925800428712,
    -5.16770687881004,
    2.550031375353375,
    -0.5980451625033413,
    0.07722010591476362,
)
COSINE = (
    0.9999999534655706,
    -4.934792858503339,
    4.058411910098915,
    -1.331880131184001,
    0.21969673041819898,
)
ZOOM = 16.0 * math.sqrt(math.log2(math.e))
VMEM = pl.BlockSpec(memory_space=pltpu.VMEM)
HBM = pl.BlockSpec(memory_space=pltpu.HBM)


def call(body, out, ins, scratch=(), flops=0, nbytes=0, trans=0, grant=16, spec=VMEM):
    multiple = isinstance(out, (list, tuple))
    return pl.pallas_call(
        body,
        out_shape=out,
        in_specs=[spec] * len(ins),
        out_specs=[VMEM] * len(out) if multiple else VMEM,
        scratch_shapes=list(scratch),
        compiler_params=pltpu.CompilerParams(vmem_limit_bytes=int(grant * (1 << 20))),
        cost_estimate=pl.CostEstimate(flops=flops, bytes_accessed=nbytes, transcendentals=trans),
    )(*ins)


def dot(left, right):
    return jnp.dot(left, right, preferred_element_type=jnp.float32)


def sine_cosine(turns):
    rest = turns - jnp.round(turns)
    square = rest * rest
    odd = SINE[-1]
    for coef in SINE[-2::-1]:
        odd = odd * square + coef
    even = COSINE[-1]
    for coef in COSINE[-2::-1]:
        even = even * square + coef
    half = odd * rest
    return 2.0 * (half * even), 1.0 - 2.0 * (half * half)


def begin_kernel(wave_hbm, place_hbm, cols, place_out, waves, place, flat, sems):
    share = cols.shape[0]
    first = pl.multiple_of(lax.axis_index("role") * share, 128)
    copies = [
        pltpu.make_async_copy(wave_hbm.at[:, pl.ds(first, share)], waves, sems.at[0]),
        pltpu.make_async_copy(place_hbm, place, sems.at[1]),
    ]
    for copy in copies:
        copy.start()
    flat[...] = jnp.zeros_like(flat)
    copies[0].wait()
    for i in range(share // 128):
        part = waves[:, i * 128 : (i + 1) * 128].astype(jnp.float32)
        for k in range(3):
            flat[3 * k : 3 * k + 3, :] = part
        cols[i * 128 : (i + 1) * 128, :] = flat[...].T.astype(jnp.bfloat16)
    copies[1].wait()
    for c in range(3):
        place_out[c : c + 1, :] = place[c]


def tables_kernel(*refs):
    pos_refs, (cols, by_wave, pos, parts) = refs[:4], refs[4:]
    atoms = pos_refs[0].shape[1]
    total = pos.shape[1]
    pos[...] = jnp.zeros_like(pos)
    for i, ref in enumerate(pos_refs):
        rest = ref[...]
        for k in range(3):
            rounded = rest.astype(jnp.bfloat16).astype(jnp.float32)
            pos[3 * k : 3 * k + 3, i * atoms : (i + 1) * atoms] = rounded
            rest = rest - rounded
    parts[...] = pos[...].astype(jnp.bfloat16)
    share = by_wave.shape[0] // 2
    step = 64

    def block(j, carry):
        waves = cols[pl.ds(pl.multiple_of(j * step, step), step), :]
        sine, cosine = sine_cosine(dot(waves, parts[...]))
        both = jnp.stack(
            [cosine.reshape(step // 8, 8, total), sine.reshape(step // 8, 8, total)], axis=1
        ).reshape(2 * step, total)
        part = pl.ds(pl.multiple_of(j * 2 * step, 2 * step), 2 * step)
        by_wave[part, :] = both.astype(jnp.bfloat16)
        return carry

    lax.fori_loop(0, share // step, block, 0)


def flip_kernel(by_wave, by_atom):
    for j in range(by_wave.shape[0] // 128):
        part = slice(j * 128, (j + 1) * 128)
        by_atom[:, part] = by_wave[part, :].T


def core_half(size, other):
    core = lax.axis_index("atoms") & 1
    core = 1 - core if other else core
    return pl.ds(pl.multiple_of(core * size, size), size)


def send_kernel(scale, *refs):
    rows_refs, (wq_ref, table, out_ref, queries) = refs[:4], refs[4:]
    atoms = rows_refs[0].shape[0]
    weight = wq_ref[...]
    for i, rows in enumerate(rows_refs):
        queries[i * atoms : (i + 1) * atoms, :] = dot(rows[...], weight).astype(jnp.bfloat16)
    part = core_half(out_ref.shape[0], True)
    out_ref[...] = (dot(table[part, :], queries[...]) * scale).astype(jnp.bfloat16)


def own_kernel(scale, queries, table, out_ref):
    part = core_half(out_ref.shape[0], False)
    out_ref[...] = dot(table[part, :], queries[...]) * scale


def keep_kernel(own_ref, got_ref, out_ref):
    out_ref[...] = (own_ref[...] + got_ref[...].astype(jnp.float32)).astype(jnp.bfloat16)


def stack_kernel(*refs):
    rows_refs, pos_refs, (out_ref, parts) = refs[:3], refs[3:6], refs[6:]
    atoms = rows_refs[0].shape[0]
    parts[...] = jnp.zeros_like(parts)
    for i in range(3):
        out_ref[i, 0:atoms, :] = rows_refs[i][...]
        rest = pos_refs[i][...]
        for k in range(3):
            rounded = rest.astype(jnp.bfloat16).astype(jnp.float32)
            parts[8 * k : 8 * k + 3, :] = rounded
            rest = rest - rounded
        out_ref[i, atoms:, :] = parts[...].astype(jnp.bfloat16)


def reduce_kernel(mine_ref, wave_ref, kgain_ref, out_ref):
    chips, rows, width = mine_ref.shape
    piece = rows // 2
    share = 2 * chips * piece
    column = lax.axis_index("atoms")
    first = lax.axis_index("role") * share + ((column & 1) * chips + (column >> 1)) * piece
    start = pl.multiple_of((first // 128) * 128, 128)
    waves = wave_ref[:, pl.ds(start, 128)].astype(jnp.float32)
    squares = jnp.broadcast_to(jnp.sum(waves * waves, axis=0, keepdims=True), (piece, 128))
    lanes = lax.broadcasted_iota(jnp.int32, (piece, 128), 1)
    wanted = lax.broadcasted_iota(jnp.int32, (piece, 128), 0) + (first - start)
    square = jnp.sum(jnp.where(lanes == wanted, squares, 0.0), axis=1, keepdims=True)
    k_filter = ewald_scale * kgain_ref[...] * (jnp.exp(-square / damping) / square)
    total = jnp.sum(mine_ref[...].astype(jnp.float32), axis=0)
    filtered = total * jnp.concatenate([k_filter, k_filter], axis=0)
    out_ref[...] = jnp.broadcast_to(filtered.astype(jnp.bfloat16)[None], (chips, rows, width))


def ewald_kernel(table_ref, own_ref, other_ref, *out_refs):
    atoms, _ = out_refs[0].shape
    size = own_ref.shape[0]
    for i, out_ref in enumerate(out_refs):
        part = slice(i * atoms, (i + 1) * atoms)
        total = dot(table_ref[part, core_half(size, False)], own_ref[...])
        total = total + dot(table_ref[part, core_half(size, True)], other_ref[...])
        out_ref[...] = total.astype(jnp.bfloat16)


def final_kernel(rows_ref, short_ref, e0_ref, e1_ref, e2_ref, e3_ref, wout_ref, out_ref):
    total = short_ref[...]
    for ref in (e0_ref, e1_ref, e2_ref, e3_ref):
        total = total + ref[...].astype(jnp.float32)
    moved = dot(total.astype(jnp.bfloat16), wout_ref[...])
    out_ref[...] = (rows_ref[...].astype(jnp.float32) + moved).astype(jnp.bfloat16)


def prepare_kernel(
    r0, r1, r2, low_ref, high_ref, p0, p1, p2, slots_ref, images_ref, win_ref, wrbf_ref, brbf_ref, wf_ref,
    hidden, cols, pairs, bias, wf_out, pos, turned,
):
    basis_count, width = wrbf_ref.shape
    pairs[...] = jnp.zeros_like(pairs)
    pairs[0:basis_count, 0:width] = wrbf_ref[...]
    pairs[basis_count:, width:] = wrbf_ref[...]
    bias[:, 0:width] = brbf_ref[...] * math.log2(math.e)
    bias[:, width:] = brbf_ref[...] * math.log2(math.e)
    wf_out[...] = wf_ref[...]
    slots, atoms = slots_ref.shape
    weight = win_ref[...]
    own = (r0, r1, r2)
    for p in range(3):
        for q in range(3):
            brick = p * 3 + q
            if q == 1:
                rows, place = own[p][...], (p0, p1, p2)[p][...]
            else:
                ref = low_ref if q == 0 else high_ref
                rows = ref[p, 0:atoms, :]
                parts = ref[p, atoms:, :].astype(jnp.float32)
                place = (parts[0:3, :] + parts[8:11, :]) + parts[16:19, :]
            hidden[brick * atoms : (brick + 1) * atoms, :] = dot(rows, weight).astype(jnp.bfloat16)
            pos[0:3, brick * atoms : (brick + 1) * atoms] = place
    lane = 128
    for half in range(atoms // lane):
        cut = slice(half * lane, (half + 1) * lane)
        index = slots_ref[:, cut]
        image = images_ref[:, cut]
        place = index & (lane - 1)
        group = index >> 7
        near = [jnp.zeros((slots, lane), jnp.float32) for _ in range(3)]
        for r in range(9 * atoms // lane):
            here = group == r
            for c in range(3):
                table = jnp.broadcast_to(pos[c : c + 1, r * lane : (r + 1) * lane], (slots, lane))
                taken = jnp.take_along_axis(table, place, axis=1, mode="promise_in_bounds")
                near[c] = jnp.where(here, taken, near[c])
        first = (image >= 9).astype(jnp.int32) + (image >= 18).astype(jnp.int32)
        inside = image - 9 * first
        second = (inside >= 3).astype(jnp.int32) + (inside >= 6).astype(jnp.int32)
        third = inside - 3 * second
        square = jnp.zeros((slots, lane), jnp.float32)
        for c, offset in enumerate((first, second, third)):
            delta = near[c] + (offset - 1).astype(jnp.float32) * box_side - p1[c : c + 1, cut]
            square = square + delta * delta
        rest = jnp.sqrt(square + soft_sq) * ZOOM
        for k in range(3):
            rounded = rest.astype(jnp.bfloat16).astype(jnp.float32)
            turned[k * slots : (k + 1) * slots, cut] = rounded
            rest = rest - rounded
        turned[3 * slots : 4 * slots, cut] = ((lane + place) << group).astype(jnp.float32)
    cols[...] = turned[...].T.astype(jnp.bfloat16)


def short_kernel(first, count, scale, cols_ref, hidden, pairs, bias, wf_ref, *refs):
    lane = 128
    atoms = cols_ref.shape[0]
    slots = cols_ref.shape[1] // 4
    basis_count, width = pairs.shape[0] // 2, wf_ref.shape[1]
    out_ref = refs[-1]
    out_ref[...] = refs[0][...] if len(refs) > 1 else jnp.zeros_like(out_ref)
    row = lax.broadcasted_iota(jnp.int32, (lane, 6 * lane), 0)
    column = lax.broadcasted_iota(jnp.int32, (lane, 6 * lane), 1)
    code_slot = jnp.where(row >= 3 * slots, row - 3 * slots - (column >> 7), -lane)
    dist_slot = jnp.where(row < 3 * slots, (row & (slots - 1)) - ((column - 4 * lane) >> 6), -lane)
    source = jnp.where(column < 4 * lane, code_slot, dist_slot)
    centers = (
        (lax.broadcasted_iota(jnp.int32, (1, lane), 1) & (basis_count - 1)).astype(jnp.float32)
        * (4.0 / (basis_count - 1))
        * ZOOM
    )
    lanes = lax.broadcasted_iota(jnp.int32, (16, lane), 1) + lane
    groups = 9 * atoms // lane

    def spread(j):
        select = (source == 4 * j).astype(jnp.float32).astype(jnp.bfloat16)
        return dot(cols_ref[...], select)

    def hot_of(wide):
        codes = [
            wide[:, i * lane : (i + 1) * lane].astype(jnp.bfloat16) for i in range(4)
        ]
        code = jnp.concatenate(codes, axis=0)
        parts = []
        for g in range(groups):
            number = jnp.broadcast_to(
                (lanes << g).astype(jnp.float32).astype(jnp.bfloat16)[None],
                (4 * atoms // 16, 16, lane),
            ).reshape(4 * atoms, lane)
            parts.append(jnp.where(code == number, jnp.bfloat16(1), jnp.bfloat16(0)))
        return jnp.concatenate(parts, axis=1)

    def filters_of(wide):
        inner = []
        for p in range(2):
            offset = wide[:, (4 + p) * lane : (5 + p) * lane] - centers
            basis = jnp.exp2(-(offset * offset)).astype(jnp.bfloat16)
            value = dot(basis, pairs[...]) * math.log2(math.e) + bias[...]
            both = (jnp.log(1.0 + jnp.exp2(value)) - math.log(2.0)).astype(jnp.bfloat16)
            inner += [both[:, :width], both[:, width:]]
        return dot(jnp.concatenate(inner, axis=0), wf_ref[...])

    def add(filters, gathered):
        product = filters * gathered
        total = product[0:atoms]
        for i in range(1, 4):
            total = total + product[i * atoms : (i + 1) * atoms]
        out_ref[...] += total

    def body(j, carry):
        wide = spread(first + j)
        gathered = dot(hot_of(wide), hidden[...])
        add(filters_of(wide), gathered)
        return carry

    lax.fori_loop(0, count, body, 0)
    out_ref[...] = out_ref[...] * scale


def block(
    features,
    positions,
    neighbours,
    images,
    wave,
    kgain,
    w_in,
    w_query,
    w_rbf,
    b_rbf,
    w_filter,
    w_out,
):
    f32, bf16 = jnp.float32, jnp.bfloat16
    rows = features[0, 0]
    atoms, width = rows.shape
    slots = neighbours.shape[2]
    roles = lax.axis_size("role")
    columns = lax.axis_size("atoms")
    atom_total = atoms * roles * columns
    waves = wave.shape[1]
    share = waves // roles
    piece = share // columns

    def from_role(block, shift):
        return lax.ppermute(block, "role", [((i + shift) % roles, i) for i in range(roles)])

    def from_column(block, shift):
        return lax.ppermute(
            block, "atoms", [((i + shift) % columns, i) for i in range(columns)]
        )

    shifts = (1, roles - 1, 2)
    order = (0,) + shifts
    wave_cols, place = call(
        begin_kernel,
        [jax.ShapeDtypeStruct((share, 128), bf16), jax.ShapeDtypeStruct((3, atoms), f32)],
        [wave, jnp.transpose(positions, (0, 2, 1, 3))[0]],
        scratch=[
            pltpu.VMEM((3, share), jnp.int32),
            pltpu.VMEM((3, 1, atoms), f32),
            pltpu.VMEM((128, 128), f32),
            pltpu.SemaphoreType.DMA((2,)),
        ],
        nbytes=1 << 19,
        grant=63.25,
        spec=HBM,
    )
    place_of = {0: place, **{d: from_role(place, d) for d in shifts}}
    rows_of = {0: rows, **{d: from_role(rows, d) for d in shifts}}
    by_wave = call(
        tables_kernel,
        jax.ShapeDtypeStruct((2 * share, roles * atoms), bf16),
        [place_of[d] for d in order] + [wave_cols],
        scratch=[pltpu.VMEM((128, roles * atoms), f32), pltpu.VMEM((128, roles * atoms), bf16)],
        flops=40 * share * roles * atoms,
        nbytes=4 << 20,
    )
    norm = atom_total ** (-0.5)
    partner = [(i, i ^ 1) for i in range(columns)]
    same_core = [list(range(c, columns, 2)) for c in range(2)]
    sent, queries = call(
        functools.partial(send_kernel, norm),
        [jax.ShapeDtypeStruct((share, width), bf16), jax.ShapeDtypeStruct((roles * atoms, width), bf16)],
        [rows_of[d] for d in order] + [w_query, by_wave],
        flops=2 * share * roles * atoms * width,
        nbytes=3 << 20,
    )
    got = lax.ppermute(sent, "atoms", partner)
    own = call(
        functools.partial(own_kernel, norm),
        jax.ShapeDtypeStruct((share, width), f32),
        [queries, by_wave],
        flops=2 * share * roles * atoms * width,
        nbytes=2 << 20,
    )
    kept = call(
        keep_kernel,
        jax.ShapeDtypeStruct((share, width), bf16),
        [own, got],
        flops=share * width,
        nbytes=1 << 20,
    )
    by_atom = call(
        flip_kernel,
        jax.ShapeDtypeStruct((roles * atoms, 2 * share), bf16),
        [by_wave],
        nbytes=4 << 20,
    )
    chunks = (columns // 2, 2 * piece, width)
    mine = lax.all_to_all(kept.reshape(chunks), "atoms", 0, 0, axis_index_groups=same_core)
    copies = call(
        reduce_kernel,
        jax.ShapeDtypeStruct(chunks, bf16),
        [mine, wave, kgain[None, :]],
        flops=2 * share * width,
        nbytes=1 << 20,
    )
    half_own = lax.all_to_all(copies, "atoms", 0, 0, axis_index_groups=same_core).reshape(
        share, width
    )
    half_other = lax.ppermute(half_own, "atoms", partner)

    triple = (roles - 1, 0, 1)
    bundle = call(
        stack_kernel,
        jax.ShapeDtypeStruct((3, atoms + 32, width), bf16),
        [rows_of[d] for d in triple] + [place_of[d] for d in triple],
        scratch=[pltpu.VMEM((32, width), f32)],
        nbytes=1 << 20,
    )
    low, high = from_column(bundle, columns - 1), from_column(bundle, 1)
    hidden, cols, pairs, bias, filter_weight = call(
        prepare_kernel,
        [
            jax.ShapeDtypeStruct((9 * atoms, width), bf16),
            jax.ShapeDtypeStruct((atoms, 4 * slots), bf16),
            jax.ShapeDtypeStruct((2 * w_rbf.shape[0], 2 * width), bf16),
            jax.ShapeDtypeStruct((1, 2 * width), f32),
            jax.ShapeDtypeStruct((width, width), bf16),
        ],
        [rows_of[d] for d in triple]
        + [low, high]
        + [place_of[d] for d in triple]
        + [neighbours[0, 0], images[0, 0], w_in, w_rbf, b_rbf[None, :], w_filter],
        scratch=[pltpu.VMEM((8, 9 * atoms), f32), pltpu.VMEM((4 * slots, atoms), f32)],
        flops=2 * 9 * atoms * width * width,
        nbytes=4 << 20,
        grant=63.25,
    )
    short = ()
    ends = (0, 2, 6, slots // 4)
    for i in range(3):
        count = ends[i + 1] - ends[i]
        short = (
            call(
                functools.partial(short_kernel, ends[i], count, 1.0 if i < 2 else slots ** (-0.5)),
                jax.ShapeDtypeStruct((atoms, width), f32),
                [cols, hidden, pairs, bias, filter_weight, *short],
                flops=2 * 4 * count * atoms * 9 * atoms * width,
                nbytes=4 << 20,
                grant=63.25 if i < 2 else 16,
            ),
        )
    short = short[0]
    parts = call(
        ewald_kernel,
        [jax.ShapeDtypeStruct((atoms, width), bf16)] * roles,
        [by_atom, half_own, half_other],
        flops=2 * 2 * share * roles * atoms * width,
        nbytes=4 << 20,
    )
    back = [parts[0]] + [from_role(parts[1 + i], roles - d) for i, d in enumerate(shifts)]
    result = call(
        final_kernel,
        jax.ShapeDtypeStruct((atoms, width), bf16),
        [rows, short] + back + [w_out],
        flops=2 * atoms * width * width,
        nbytes=1 << 20,
    )
    return result[None, None]


def solution(mesh):
    in_specs = (
        P("role", "atoms", None, None),
        P("role", "atoms", None, None),
        P("role", "atoms", None, None),
        P("role", "atoms", None, None),
        P(),
        P(),
        P(),
        P(),
        P(),
        P(),
        P(),
        P(),
    )
    out_specs = P("role", "atoms", None, None)
    return jax.shard_map(block, mesh=mesh, in_specs=in_specs, out_specs=out_specs, check_vma=False)
```

```python
import functools
import math

import jax
import jax.numpy as jnp
from jax import lax
from jax.experimental import pallas as pl
from jax.experimental.pallas import tpu as pltpu
from jax.sharding import PartitionSpec as P


box_side = 1.0
soft_sq = 0.01
damping = 64.0
ewald_scale = 0.25
SINE = (
    3.1415925800428712,
    -5.16770687881004,
    2.550031375353375,
    -0.5980451625033413,
    0.07722010591476362,
)
COSINE = (
    0.9999999534655706,
    -4.934792858503339,
    4.058411910098915,
    -1.331880131184001,
    0.21969673041819898,
)
ZOOM = 16.0 * math.sqrt(math.log2(math.e))
VMEM = pl.BlockSpec(memory_space=pltpu.VMEM)
HBM = pl.BlockSpec(memory_space=pltpu.HBM)


def call(body, out, ins, scratch=(), flops=0, nbytes=0, trans=0, grant=16, spec=None):
    multiple = isinstance(out, (list, tuple))
    return pl.pallas_call(
        body,
        out_shape=out,
        in_specs=spec or [VMEM] * len(ins),
        out_specs=[VMEM] * len(out) if multiple else VMEM,
        scratch_shapes=list(scratch),
        compiler_params=pltpu.CompilerParams(vmem_limit_bytes=int(grant * (1 << 20))),
        cost_estimate=pl.CostEstimate(flops=flops, bytes_accessed=nbytes, transcendentals=trans),
    )(*ins)


def dot(left, right):
    return jnp.dot(left, right, preferred_element_type=jnp.float32)


def sine_cosine(turns):
    rest = turns - jnp.round(turns)
    square = rest * rest
    odd = SINE[-1]
    for coef in SINE[-2::-1]:
        odd = odd * square + coef
    even = COSINE[-1]
    for coef in COSINE[-2::-1]:
        even = even * square + coef
    half = odd * rest
    return 2.0 * (half * even), 1.0 - 2.0 * (half * half)


def begin_kernel(wave_hbm, place_hbm, cols, place_out, waves, place, flat, sems):
    share = cols.shape[0]
    first = pl.multiple_of(lax.axis_index("role") * share, 128)
    copies = [
        pltpu.make_async_copy(wave_hbm.at[:, pl.ds(first, share)], waves, sems.at[0]),
        pltpu.make_async_copy(place_hbm, place, sems.at[1]),
    ]
    for copy in copies:
        copy.start()
    flat[...] = jnp.zeros_like(flat)
    copies[0].wait()
    for i in range(share // 128):
        part = waves[:, i * 128 : (i + 1) * 128].astype(jnp.float32)
        for k in range(3):
            flat[3 * k : 3 * k + 3, :] = part
        cols[i * 128 : (i + 1) * 128, :] = flat[...].T.astype(jnp.bfloat16)
    copies[1].wait()
    for c in range(3):
        place_out[c : c + 1, :] = place[c]


def tables_kernel(*refs):
    pos_refs, (cols, by_wave, pos, parts) = refs[:4], refs[4:]
    atoms = pos_refs[0].shape[1]
    total = pos.shape[1]
    pos[...] = jnp.zeros_like(pos)
    for i, ref in enumerate(pos_refs):
        rest = ref[...]
        for k in range(3):
            rounded = rest.astype(jnp.bfloat16).astype(jnp.float32)
            pos[3 * k : 3 * k + 3, i * atoms : (i + 1) * atoms] = rounded
            rest = rest - rounded
    parts[...] = pos[...].astype(jnp.bfloat16)
    share = by_wave.shape[0] // 2
    step = 64

    def block(j, carry):
        waves = cols[pl.ds(pl.multiple_of(j * step, step), step), :]
        sine, cosine = sine_cosine(dot(waves, parts[...]))
        both = jnp.stack(
            [cosine.reshape(step // 8, 8, total), sine.reshape(step // 8, 8, total)], axis=1
        ).reshape(2 * step, total)
        part = pl.ds(pl.multiple_of(j * 2 * step, 2 * step), 2 * step)
        by_wave[part, :] = both.astype(jnp.bfloat16)
        return carry

    lax.fori_loop(0, share // step, block, 0)


def flip_kernel(by_wave, by_atom):
    for j in range(by_wave.shape[0] // 128):
        part = slice(j * 128, (j + 1) * 128)
        by_atom[:, part] = by_wave[part, :].T


def core_half(size, other):
    core = lax.axis_index("atoms") & 1
    core = 1 - core if other else core
    return pl.ds(pl.multiple_of(core * size, size), size)


def send_kernel(scale, *refs):
    rows_refs, (wq_ref, table, out_ref, queries) = refs[:4], refs[4:]
    atoms = rows_refs[0].shape[0]
    weight = wq_ref[...]
    for i, rows in enumerate(rows_refs):
        queries[i * atoms : (i + 1) * atoms, :] = dot(rows[...], weight).astype(jnp.bfloat16)
    part = core_half(out_ref.shape[0], True)
    out_ref[...] = (dot(table[part, :], queries[...]) * scale).astype(jnp.bfloat16)


def own_kernel(scale, queries, table, out_ref):
    part = core_half(out_ref.shape[0], False)
    out_ref[...] = dot(table[part, :], queries[...]) * scale


def keep_kernel(own_ref, got_ref, out_ref):
    out_ref[...] = (own_ref[...] + got_ref[...].astype(jnp.float32)).astype(jnp.bfloat16)


def stack_kernel(*refs):
    rows_refs, pos_refs, (out_ref, parts) = refs[:3], refs[3:6], refs[6:]
    atoms = rows_refs[0].shape[0]
    parts[...] = jnp.zeros_like(parts)
    for i in range(3):
        out_ref[i, 0:atoms, :] = rows_refs[i][...]
        rest = pos_refs[i][...]
        for k in range(3):
            rounded = rest.astype(jnp.bfloat16).astype(jnp.float32)
            parts[8 * k : 8 * k + 3, :] = rounded
            rest = rest - rounded
        out_ref[i, atoms:, :] = parts[...].astype(jnp.bfloat16)


def reduce_kernel(mine_ref, wave_ref, kgain_ref, out_ref):
    chips, rows, width = mine_ref.shape
    piece = rows // 2
    share = 2 * chips * piece
    column = lax.axis_index("atoms")
    first = lax.axis_index("role") * share + ((column & 1) * chips + (column >> 1)) * piece
    start = pl.multiple_of((first // 128) * 128, 128)
    waves = wave_ref[:, pl.ds(start, 128)].astype(jnp.float32)
    squares = jnp.broadcast_to(jnp.sum(waves * waves, axis=0, keepdims=True), (piece, 128))
    lanes = lax.broadcasted_iota(jnp.int32, (piece, 128), 1)
    wanted = lax.broadcasted_iota(jnp.int32, (piece, 128), 0) + (first - start)
    square = jnp.sum(jnp.where(lanes == wanted, squares, 0.0), axis=1, keepdims=True)
    k_filter = ewald_scale * kgain_ref[...] * (jnp.exp(-square / damping) / square)
    total = jnp.sum(mine_ref[...].astype(jnp.float32), axis=0)
    filtered = total * jnp.concatenate([k_filter, k_filter], axis=0)
    out_ref[...] = jnp.broadcast_to(filtered.astype(jnp.bfloat16)[None], (chips, rows, width))


def ewald_kernel(table_ref, own_ref, other_ref, *out_refs):
    atoms, _ = out_refs[0].shape
    size = own_ref.shape[0]
    for i, out_ref in enumerate(out_refs):
        part = slice(i * atoms, (i + 1) * atoms)
        total = dot(table_ref[part, core_half(size, False)], own_ref[...])
        total = total + dot(table_ref[part, core_half(size, True)], other_ref[...])
        out_ref[...] = total.astype(jnp.bfloat16)


def final_kernel(rows_ref, short_ref, e0_ref, e1_ref, e2_ref, e3_ref, wout_ref, out_ref):
    total = short_ref[...]
    for ref in (e0_ref, e1_ref, e2_ref, e3_ref):
        total = total + ref[...].astype(jnp.float32)
    moved = dot(total.astype(jnp.bfloat16), wout_ref[...])
    out_ref[...] = (rows_ref[...].astype(jnp.float32) + moved).astype(jnp.bfloat16)


def prepare_kernel(
    r0, r1, r2, low_ref, high_ref, p0, p1, p2, slots_ref, images_ref, win_ref, wrbf_ref, brbf_ref,
    table, cols, pairs, bias, row_at, pos, turned,
):
    basis_count, width = wrbf_ref.shape
    pairs[...] = jnp.zeros_like(pairs)
    pairs[0:basis_count, 0:width] = wrbf_ref[...]
    pairs[basis_count:, width:] = wrbf_ref[...]
    bias[:, 0:width] = brbf_ref[...] * math.log2(math.e)
    bias[:, width:] = brbf_ref[...] * math.log2(math.e)
    lane = 128
    halves = width // lane
    slots, atoms = slots_ref.shape
    weight = win_ref[...]
    own = (r0, r1, r2)
    for p in range(3):
        for q in range(3):
            brick = p * 3 + q
            if q == 1:
                rows, place = own[p][...], (p0, p1, p2)[p][...]
            else:
                ref = low_ref if q == 0 else high_ref
                rows = ref[p, 0:atoms, :]
                parts = ref[p, atoms:, :].astype(jnp.float32)
                place = (parts[0:3, :] + parts[8:11, :]) + parts[16:19, :]
            hidden = dot(rows, weight).astype(jnp.bfloat16).astype(jnp.float32)
            for h in range(halves):
                table[pl.ds(halves * brick * atoms + h, atoms, stride=halves), :] = hidden[
                    :, h * lane : (h + 1) * lane
                ]
            pos[0:3, brick * atoms : (brick + 1) * atoms] = place
    row_at[...] = slots_ref[...] * halves
    table[halves * 9 * atoms :, :] = jnp.zeros((table.shape[0] - halves * 9 * atoms, lane), jnp.float32)
    for half in range(atoms // lane):
        cut = slice(half * lane, (half + 1) * lane)
        index = slots_ref[:, cut]
        image = images_ref[:, cut]
        place = index & (lane - 1)
        group = index >> 7
        near = [jnp.zeros((slots, lane), jnp.float32) for _ in range(3)]
        for r in range(9 * atoms // lane):
            here = group == r
            for c in range(3):
                table = jnp.broadcast_to(pos[c : c + 1, r * lane : (r + 1) * lane], (slots, lane))
                taken = jnp.take_along_axis(table, place, axis=1, mode="promise_in_bounds")
                near[c] = jnp.where(here, taken, near[c])
        first = (image >= 9).astype(jnp.int32) + (image >= 18).astype(jnp.int32)
        inside = image - 9 * first
        second = (inside >= 3).astype(jnp.int32) + (inside >= 6).astype(jnp.int32)
        third = inside - 3 * second
        square = jnp.zeros((slots, lane), jnp.float32)
        for c, offset in enumerate((first, second, third)):
            delta = near[c] + (offset - 1).astype(jnp.float32) * box_side - p1[c : c + 1, cut]
            square = square + delta * delta
        rest = jnp.sqrt(square + soft_sq) * ZOOM
        for k in range(3):
            rounded = rest.astype(jnp.bfloat16).astype(jnp.float32)
            turned[k * slots : (k + 1) * slots, cut] = rounded
            rest = rest - rounded
        turned[3 * slots : 4 * slots, cut] = jnp.zeros((slots, lane), jnp.float32)
    cols[...] = turned[...].T.astype(jnp.bfloat16)


def short_kernel(
    scale, cols_ref, table, row_at, pairs, bias, wf_ref, out_ref, near_a, near_b, at_a, at_b, sems
):
    lane = 128
    atoms = cols_ref.shape[0]
    slots = cols_ref.shape[1] // 4
    basis_count, width = pairs.shape[0] // 2, wf_ref.shape[1]
    halves = width // lane
    group = near_a.shape[0] // (halves * atoms)
    ahead = at_a.shape[0]
    wide_lanes = group // 2 * lane
    out_ref[...] = jnp.zeros_like(out_ref)
    row = lax.broadcasted_iota(jnp.int32, (lane, wide_lanes), 0)
    column = lax.broadcasted_iota(jnp.int32, (lane, wide_lanes), 1)
    source = jnp.where(row < 3 * slots, (row & (slots - 1)) - (column >> 6), -lane)
    centers = (
        (lax.broadcasted_iota(jnp.int32, (1, lane), 1) & (basis_count - 1)).astype(jnp.float32)
        * (4.0 / (basis_count - 1))
        * ZOOM
    )

    def fetch(first, buffer, sem):
        rows = pl.ds(pl.multiple_of(first, ahead), ahead)
        return pltpu.make_async_copy(row_at.at[rows, :], buffer, sem)

    def one_group(first, buffer, offset, near):
        for i in range(group):
            for k in range(atoms):
                to = (i * atoms + k) * halves
                near[to : to + halves, :] = table[pl.ds(buffer[offset + i, k], halves), :]
        select = (source == first).astype(jnp.float32).astype(jnp.bfloat16)
        wide = dot(cols_ref[...], select)
        inner = []
        for p in range(group // 2):
            offset = wide[:, p * lane : (p + 1) * lane] - centers
            basis = jnp.exp2(-(offset * offset)).astype(jnp.bfloat16)
            value = dot(basis, pairs[...]) * math.log2(math.e) + bias[...]
            both = (jnp.log(1.0 + jnp.exp2(value)) - math.log(2.0)).astype(jnp.bfloat16)
            inner += [both[:, :width], both[:, width:]]
        filters = dot(jnp.concatenate(inner, axis=0), wf_ref[...])
        for h in range(halves):
            cut = slice(h * lane, (h + 1) * lane)
            total = out_ref[:, cut]
            for i in range(group):
                gathered = near[pl.ds(i * atoms * halves + h, atoms, stride=halves), :]
                total = total + filters[i * atoms : (i + 1) * atoms, cut] * gathered
            out_ref[:, cut] = total

    def both_groups(first, buffer):
        one_group(first, buffer, 0, near_a)
        one_group(first + group, buffer, group, near_b)

    fetch(0, at_a, sems.at[0]).start()

    def body(j, carry):
        first = 2 * ahead * j
        fetch(first, at_a, sems.at[0]).wait()
        fetch(first + ahead, at_b, sems.at[1]).start()
        both_groups(first, at_a)
        fetch(first + ahead, at_b, sems.at[1]).wait()

        @pl.when(first + 2 * ahead < slots)
        def _():
            fetch(first + 2 * ahead, at_a, sems.at[0]).start()

        both_groups(first + ahead, at_b)
        return carry

    lax.fori_loop(0, slots // (2 * ahead), body, 0)
    out_ref[...] = out_ref[...] * scale


def block(
    features,
    positions,
    neighbours,
    images,
    wave,
    kgain,
    w_in,
    w_query,
    w_rbf,
    b_rbf,
    w_filter,
    w_out,
):
    f32, bf16 = jnp.float32, jnp.bfloat16
    rows = features[0, 0]
    atoms, width = rows.shape
    slots = neighbours.shape[2]
    roles = lax.axis_size("role")
    columns = lax.axis_size("atoms")
    atom_total = atoms * roles * columns
    waves = wave.shape[1]
    share = waves // roles
    piece = share // columns

    def from_role(block, shift):
        return lax.ppermute(block, "role", [((i + shift) % roles, i) for i in range(roles)])

    def from_column(block, shift):
        return lax.ppermute(
            block, "atoms", [((i + shift) % columns, i) for i in range(columns)]
        )

    shifts = (1, roles - 1, 2)
    order = (0,) + shifts
    wave_cols, place = call(
        begin_kernel,
        [jax.ShapeDtypeStruct((share, 128), bf16), jax.ShapeDtypeStruct((3, atoms), f32)],
        [wave, jnp.transpose(positions, (0, 2, 1, 3))[0]],
        scratch=[
            pltpu.VMEM((3, share), jnp.int32),
            pltpu.VMEM((3, 1, atoms), f32),
            pltpu.VMEM((128, 128), f32),
            pltpu.SemaphoreType.DMA((2,)),
        ],
        nbytes=1 << 19,
        grant=63.25,
        spec=[HBM] * 2,
    )
    place_of = {0: place, **{d: from_role(place, d) for d in shifts}}
    rows_of = {0: rows, **{d: from_role(rows, d) for d in shifts}}
    by_wave = call(
        tables_kernel,
        jax.ShapeDtypeStruct((2 * share, roles * atoms), bf16),
        [place_of[d] for d in order] + [wave_cols],
        scratch=[pltpu.VMEM((128, roles * atoms), f32), pltpu.VMEM((128, roles * atoms), bf16)],
        flops=40 * share * roles * atoms,
        nbytes=4 << 20,
    )
    norm = atom_total ** (-0.5)
    partner = [(i, i ^ 1) for i in range(columns)]
    same_core = [list(range(c, columns, 2)) for c in range(2)]
    sent, queries = call(
        functools.partial(send_kernel, norm),
        [jax.ShapeDtypeStruct((share, width), bf16), jax.ShapeDtypeStruct((roles * atoms, width), bf16)],
        [rows_of[d] for d in order] + [w_query, by_wave],
        flops=2 * share * roles * atoms * width,
        nbytes=3 << 20,
    )
    got = lax.ppermute(sent, "atoms", partner)
    own = call(
        functools.partial(own_kernel, norm),
        jax.ShapeDtypeStruct((share, width), f32),
        [queries, by_wave],
        flops=2 * share * roles * atoms * width,
        nbytes=2 << 20,
    )
    kept = call(
        keep_kernel,
        jax.ShapeDtypeStruct((share, width), bf16),
        [own, got],
        flops=share * width,
        nbytes=1 << 20,
    )
    by_atom = call(
        flip_kernel,
        jax.ShapeDtypeStruct((roles * atoms, 2 * share), bf16),
        [by_wave],
        nbytes=4 << 20,
    )
    chunks = (columns // 2, 2 * piece, width)
    mine = lax.all_to_all(kept.reshape(chunks), "atoms", 0, 0, axis_index_groups=same_core)
    copies = call(
        reduce_kernel,
        jax.ShapeDtypeStruct(chunks, bf16),
        [mine, wave, kgain[None, :]],
        flops=2 * share * width,
        nbytes=1 << 20,
    )
    half_own = lax.all_to_all(copies, "atoms", 0, 0, axis_index_groups=same_core).reshape(
        share, width
    )
    half_other = lax.ppermute(half_own, "atoms", partner)

    triple = (roles - 1, 0, 1)
    bundle = call(
        stack_kernel,
        jax.ShapeDtypeStruct((3, atoms + 32, width), bf16),
        [rows_of[d] for d in triple] + [place_of[d] for d in triple],
        scratch=[pltpu.VMEM((32, width), f32)],
        nbytes=1 << 20,
    )
    low, high = from_column(bundle, columns - 1), from_column(bundle, 1)
    table, cols, pairs, bias, row_at = call(
        prepare_kernel,
        [
            jax.ShapeDtypeStruct((9 * atoms * width // 128 + 16, 128), f32),
            jax.ShapeDtypeStruct((atoms, 4 * slots), bf16),
            jax.ShapeDtypeStruct((2 * w_rbf.shape[0], 2 * width), bf16),
            jax.ShapeDtypeStruct((1, 2 * width), f32),
            jax.ShapeDtypeStruct((slots, atoms), jnp.int32),
        ],
        [rows_of[d] for d in triple]
        + [low, high]
        + [place_of[d] for d in triple]
        + [neighbours[0, 0], images[0, 0], w_in, w_rbf, b_rbf[None, :]],
        scratch=[pltpu.VMEM((8, 9 * atoms), f32), pltpu.VMEM((4 * slots, atoms), f32)],
        flops=2 * 9 * atoms * width * width,
        nbytes=4 << 20,
    )
    near = pltpu.VMEM((4 * atoms * width // 128, 128), f32)
    short = call(
        functools.partial(short_kernel, slots ** (-0.5)),
        jax.ShapeDtypeStruct((atoms, width), f32),
        [cols, table, row_at, pairs, bias, w_filter],
        scratch=[near, near]
        + [pltpu.SMEM((8, atoms), jnp.int32)] * 2
        + [pltpu.SemaphoreType.DMA((2,))],
        flops=4 * slots * atoms * width * width,
        nbytes=4 << 20,
    )
    parts = call(
        ewald_kernel,
        [jax.ShapeDtypeStruct((atoms, width), bf16)] * roles,
        [by_atom, half_own, half_other],
        flops=2 * 2 * share * roles * atoms * width,
        nbytes=4 << 20,
    )
    back = [parts[0]] + [from_role(parts[1 + i], roles - d) for i, d in enumerate(shifts)]
    result = call(
        final_kernel,
        jax.ShapeDtypeStruct((atoms, width), bf16),
        [rows, short] + back + [w_out],
        flops=2 * atoms * width * width,
        nbytes=1 << 20,
    )
    return result[None, None]


def solution(mesh):
    in_specs = (
        P("role", "atoms", None, None),
        P("role", "atoms", None, None),
        P("role", "atoms", None, None),
        P("role", "atoms", None, None),
        P(),
        P(),
        P(),
        P(),
        P(),
        P(),
        P(),
        P(),
    )
    out_specs = P("role", "atoms", None, None)
    return jax.shard_map(block, mesh=mesh, in_specs=in_specs, out_specs=out_specs, check_vma=False)
```

```python
import functools
import math

import jax
import jax.numpy as jnp
from jax import lax
from jax.experimental import pallas as pl
from jax.experimental.pallas import tpu as pltpu
from jax.sharding import PartitionSpec as P


box_side = 1.0
soft_sq = 0.01
damping = 64.0
ewald_scale = 0.25
SINE = (3.1415820220239103, -5.167142791318864, 2.541898979237898, -0.5546360684015085)
COSINE = (
    0.9999999534655706,
    -4.934792858503339,
    4.058411910098915,
    -1.331880131184001,
    0.21969673041819898,
)
ZOOM = 16.0 * math.sqrt(math.log2(math.e))
VMEM = pl.BlockSpec(memory_space=pltpu.VMEM)
HBM = pl.BlockSpec(memory_space=pltpu.HBM)


def call(body, out, ins, scratch=(), flops=0, nbytes=0, trans=0, grant=16, spec=None):
    multiple = isinstance(out, (list, tuple))
    return pl.pallas_call(
        body,
        out_shape=out,
        in_specs=spec or [VMEM] * len(ins),
        out_specs=[VMEM] * len(out) if multiple else VMEM,
        scratch_shapes=list(scratch),
        compiler_params=pltpu.CompilerParams(vmem_limit_bytes=int(grant * (1 << 20))),
        cost_estimate=pl.CostEstimate(flops=flops, bytes_accessed=nbytes, transcendentals=trans),
    )(*ins)


def dot(left, right):
    return jnp.dot(left, right, preferred_element_type=jnp.float32)


def sine_cosine(turns):
    rest = turns - jnp.round(turns)
    square = rest * rest
    odd = SINE[-1]
    for coef in SINE[-2::-1]:
        odd = odd * square + coef
    even = COSINE[-1]
    for coef in COSINE[-2::-1]:
        even = even * square + coef
    half = odd * rest
    return 2.0 * (half * even), 1.0 - 2.0 * (half * half)


def begin_kernel(wave_hbm, place_hbm, cols, place_out, waves, place, flat, sems):
    share = cols.shape[0]
    first = pl.multiple_of(lax.axis_index("role") * share, 128)
    copies = [
        pltpu.make_async_copy(wave_hbm.at[:, pl.ds(first, share)], waves, sems.at[0]),
        pltpu.make_async_copy(place_hbm, place, sems.at[1]),
    ]
    for copy in copies:
        copy.start()
    flat[...] = jnp.zeros_like(flat)
    copies[0].wait()
    for i in range(share // 128):
        part = waves[:, i * 128 : (i + 1) * 128].astype(jnp.float32)
        for k in range(3):
            flat[3 * k : 3 * k + 3, :] = part
        cols[i * 128 : (i + 1) * 128, :] = flat[...].T.astype(jnp.bfloat16)
    copies[1].wait()
    for c in range(3):
        place_out[c : c + 1, :] = place[c]


def tables_kernel(*refs):
    pos_refs, (cols, by_wave, pos, parts) = refs[:4], refs[4:]
    atoms = pos_refs[0].shape[1]
    total = pos.shape[1]
    pos[...] = jnp.zeros_like(pos)
    for i, ref in enumerate(pos_refs):
        rest = ref[...]
        for k in range(3):
            rounded = rest.astype(jnp.bfloat16).astype(jnp.float32)
            pos[3 * k : 3 * k + 3, i * atoms : (i + 1) * atoms] = rounded
            rest = rest - rounded
    parts[...] = pos[...].astype(jnp.bfloat16)
    share = by_wave.shape[0] // 2
    step = 64

    def block(j, carry):
        waves = cols[pl.ds(pl.multiple_of(j * step, step), step), :]
        sine, cosine = sine_cosine(dot(waves, parts[...]))
        both = jnp.stack(
            [cosine.reshape(step // 8, 8, total), sine.reshape(step // 8, 8, total)], axis=1
        ).reshape(2 * step, total)
        part = pl.ds(pl.multiple_of(j * 2 * step, 2 * step), 2 * step)
        by_wave[part, :] = both.astype(jnp.bfloat16)
        return carry

    lax.fori_loop(0, share // step, block, 0)


def flip_kernel(by_wave, by_atom):
    for j in range(by_wave.shape[0] // 128):
        part = slice(j * 128, (j + 1) * 128)
        by_atom[:, part] = by_wave[part, :].T


def core_half(size, other):
    core = lax.axis_index("atoms") & 1
    core = 1 - core if other else core
    return pl.ds(pl.multiple_of(core * size, size), size)


def send_kernel(scale, *refs):
    rows_refs, (wq_ref, table, out_ref, queries) = refs[:4], refs[4:]
    atoms = rows_refs[0].shape[0]
    weight = wq_ref[...]
    for i, rows in enumerate(rows_refs):
        queries[i * atoms : (i + 1) * atoms, :] = dot(rows[...], weight).astype(jnp.bfloat16)
    part = core_half(out_ref.shape[0], True)
    out_ref[...] = (dot(table[part, :], queries[...]) * scale).astype(jnp.bfloat16)


def own_kernel(scale, queries, table, out_ref):
    part = core_half(out_ref.shape[0], False)
    out_ref[...] = dot(table[part, :], queries[...]) * scale


def keep_kernel(own_ref, got_ref, out_ref):
    out_ref[...] = (own_ref[...] + got_ref[...].astype(jnp.float32)).astype(jnp.bfloat16)


def stack_kernel(*refs):
    rows_refs, pos_refs, (out_ref, parts) = refs[:3], refs[3:6], refs[6:]
    atoms = rows_refs[0].shape[0]
    parts[...] = jnp.zeros_like(parts)
    for i in range(3):
        out_ref[i, 0:atoms, :] = rows_refs[i][...]
        rest = pos_refs[i][...]
        for k in range(3):
            rounded = rest.astype(jnp.bfloat16).astype(jnp.float32)
            parts[8 * k : 8 * k + 3, :] = rounded
            rest = rest - rounded
        out_ref[i, atoms:, :] = parts[...].astype(jnp.bfloat16)


def reduce_kernel(mine_ref, wave_ref, kgain_ref, out_ref):
    chips, rows, width = mine_ref.shape
    piece = rows // 2
    share = 2 * chips * piece
    column = lax.axis_index("atoms")
    first = lax.axis_index("role") * share + ((column & 1) * chips + (column >> 1)) * piece
    start = pl.multiple_of((first // 128) * 128, 128)
    waves = wave_ref[:, pl.ds(start, 128)].astype(jnp.float32)
    squares = jnp.broadcast_to(jnp.sum(waves * waves, axis=0, keepdims=True), (piece, 128))
    lanes = lax.broadcasted_iota(jnp.int32, (piece, 128), 1)
    wanted = lax.broadcasted_iota(jnp.int32, (piece, 128), 0) + (first - start)
    square = jnp.sum(jnp.where(lanes == wanted, squares, 0.0), axis=1, keepdims=True)
    k_filter = ewald_scale * kgain_ref[...] * (jnp.exp(-square / damping) / square)
    total = jnp.sum(mine_ref[...].astype(jnp.float32), axis=0)
    filtered = total * jnp.concatenate([k_filter, k_filter], axis=0)
    out_ref[...] = jnp.broadcast_to(filtered.astype(jnp.bfloat16)[None], (chips, rows, width))


def ewald_kernel(table_ref, own_ref, other_ref, *out_refs):
    atoms, _ = out_refs[0].shape
    size = own_ref.shape[0]
    for i, out_ref in enumerate(out_refs):
        part = slice(i * atoms, (i + 1) * atoms)
        total = dot(table_ref[part, core_half(size, False)], own_ref[...])
        total = total + dot(table_ref[part, core_half(size, True)], other_ref[...])
        out_ref[...] = total.astype(jnp.bfloat16)


def final_kernel(rows_ref, short_ref, e0_ref, e1_ref, e2_ref, e3_ref, wout_ref, out_ref):
    total = short_ref[...]
    for ref in (e0_ref, e1_ref, e2_ref, e3_ref):
        total = total + ref[...].astype(jnp.float32)
    moved = dot(total.astype(jnp.bfloat16), wout_ref[...])
    out_ref[...] = (rows_ref[...].astype(jnp.float32) + moved).astype(jnp.bfloat16)


def prepare_kernel(
    r0, r1, r2, low_ref, high_ref, p0, p1, p2, slots_ref, images_ref, win_ref, wrbf_ref, brbf_ref, wf_ref,
    table, cols, pairs, bias, row_at, wf_out, pos, turned,
):
    basis_count, width = wrbf_ref.shape
    pairs[...] = jnp.zeros_like(pairs)
    pairs[0:basis_count, 0:width] = wrbf_ref[...]
    pairs[basis_count:, width:] = wrbf_ref[...]
    bias[:, 0:width] = brbf_ref[...] * math.log2(math.e)
    bias[:, width:] = brbf_ref[...] * math.log2(math.e)
    lane = 128
    halves = width // lane
    slots, atoms = slots_ref.shape
    weight = win_ref[...]
    own = (r0, r1, r2)
    for p in range(3):
        for q in range(3):
            brick = p * 3 + q
            if q == 1:
                rows, place = own[p][...], (p0, p1, p2)[p][...]
            else:
                ref = low_ref if q == 0 else high_ref
                rows = ref[p, 0:atoms, :]
                parts = ref[p, atoms:, :].astype(jnp.float32)
                place = (parts[0:3, :] + parts[8:11, :]) + parts[16:19, :]
            hidden = dot(rows, weight).astype(jnp.bfloat16).astype(jnp.float32)
            for h in range(halves):
                table[pl.ds(halves * brick * atoms + h, atoms, stride=halves), :] = hidden[
                    :, h * lane : (h + 1) * lane
                ]
            pos[0:3, brick * atoms : (brick + 1) * atoms] = place
    row_at[...] = slots_ref[...] * halves
    wf_out[...] = wf_ref[...]
    table[halves * 9 * atoms :, :] = jnp.zeros((table.shape[0] - halves * 9 * atoms, lane), jnp.float32)
    for half in range(atoms // lane):
        cut = slice(half * lane, (half + 1) * lane)
        index = slots_ref[:, cut]
        image = images_ref[:, cut]
        place = index & (lane - 1)
        group = index >> 7
        near = [jnp.zeros((slots, lane), jnp.float32) for _ in range(3)]
        for r in range(9 * atoms // lane):
            here = group == r
            for c in range(3):
                table = jnp.broadcast_to(pos[c : c + 1, r * lane : (r + 1) * lane], (slots, lane))
                taken = jnp.take_along_axis(table, place, axis=1, mode="promise_in_bounds")
                near[c] = jnp.where(here, taken, near[c])
        first = (image >= 9).astype(jnp.int32) + (image >= 18).astype(jnp.int32)
        inside = image - 9 * first
        second = (inside >= 3).astype(jnp.int32) + (inside >= 6).astype(jnp.int32)
        third = inside - 3 * second
        square = jnp.zeros((slots, lane), jnp.float32)
        for c, offset in enumerate((first, second, third)):
            delta = near[c] + (offset - 1).astype(jnp.float32) * box_side - p1[c : c + 1, cut]
            square = square + delta * delta
        rest = jnp.sqrt(square + soft_sq) * ZOOM
        for k in range(3):
            rounded = rest.astype(jnp.bfloat16).astype(jnp.float32)
            turned[k * slots : (k + 1) * slots, cut] = rounded
            rest = rest - rounded
        turned[3 * slots : 4 * slots, cut] = jnp.zeros((slots, lane), jnp.float32)
    cols[...] = turned[...].T.astype(jnp.bfloat16)


def short_kernel(start, count, scale, cols_ref, table, row_at, pairs, bias, wf_ref, *refs):
    lane = 128
    atoms = cols_ref.shape[0]
    slots = cols_ref.shape[1] // 4
    basis_count, width = pairs.shape[0] // 2, wf_ref.shape[1]
    halves = width // lane
    *before, out_ref, near_a, near_b, at_a, at_b, sems = refs
    group = near_a.shape[0] // (halves * atoms)
    ahead = at_a.shape[0]
    wide_lanes = group // 2 * lane
    out_ref[...] = before[0][...] if before else jnp.zeros_like(out_ref)
    row = lax.broadcasted_iota(jnp.int32, (lane, wide_lanes), 0)
    column = lax.broadcasted_iota(jnp.int32, (lane, wide_lanes), 1)
    source = jnp.where(row < 3 * slots, (row & (slots - 1)) - (column >> 6), -lane)
    centers = (
        (lax.broadcasted_iota(jnp.int32, (1, lane), 1) & (basis_count - 1)).astype(jnp.float32)
        * (4.0 / (basis_count - 1))
        * ZOOM
    )

    def fetch(first, buffer, sem):
        rows = pl.ds(pl.multiple_of(first, ahead), ahead)
        return pltpu.make_async_copy(row_at.at[rows, :], buffer, sem)

    def one_group(first, buffer, offset, near):
        for i in range(group):
            for k in range(atoms):
                to = (i * atoms + k) * halves
                near[to : to + halves, :] = table[pl.ds(buffer[offset + i, k], halves), :]
        select = (source == first).astype(jnp.float32).astype(jnp.bfloat16)
        wide = dot(cols_ref[...], select)
        inner = []
        for p in range(group // 2):
            offset = wide[:, p * lane : (p + 1) * lane] - centers
            basis = jnp.exp2(-(offset * offset)).astype(jnp.bfloat16)
            value = dot(basis, pairs[...]) * math.log2(math.e) + bias[...]
            both = (jnp.log(1.0 + jnp.exp2(value)) - math.log(2.0)).astype(jnp.bfloat16)
            inner += [both[:, :width], both[:, width:]]
        filters = dot(jnp.concatenate(inner, axis=0), wf_ref[...])
        for h in range(halves):
            cut = slice(h * lane, (h + 1) * lane)
            total = out_ref[:, cut]
            for i in range(group):
                gathered = near[pl.ds(i * atoms * halves + h, atoms, stride=halves), :]
                total = total + filters[i * atoms : (i + 1) * atoms, cut] * gathered
            out_ref[:, cut] = total

    def both_groups(first, buffer):
        one_group(first, buffer, 0, near_a)
        one_group(first + group, buffer, group, near_b)

    fetch(start, at_a, sems.at[0]).start()

    def body(j, carry):
        first = start + 2 * ahead * j
        fetch(first, at_a, sems.at[0]).wait()
        fetch(first + ahead, at_b, sems.at[1]).start()
        both_groups(first, at_a)
        fetch(first + ahead, at_b, sems.at[1]).wait()

        @pl.when(first + 2 * ahead < start + count)
        def _():
            fetch(first + 2 * ahead, at_a, sems.at[0]).start()

        both_groups(first + ahead, at_b)
        return carry

    lax.fori_loop(0, count // (2 * ahead), body, 0)
    out_ref[...] = out_ref[...] * scale


def block(
    features,
    positions,
    neighbours,
    images,
    wave,
    kgain,
    w_in,
    w_query,
    w_rbf,
    b_rbf,
    w_filter,
    w_out,
):
    f32, bf16 = jnp.float32, jnp.bfloat16
    rows = features[0, 0]
    atoms, width = rows.shape
    slots = neighbours.shape[2]
    roles = lax.axis_size("role")
    columns = lax.axis_size("atoms")
    atom_total = atoms * roles * columns
    waves = wave.shape[1]
    share = waves // roles
    piece = share // columns

    def from_role(block, shift):
        return lax.ppermute(block, "role", [((i + shift) % roles, i) for i in range(roles)])

    def from_column(block, shift):
        return lax.ppermute(
            block, "atoms", [((i + shift) % columns, i) for i in range(columns)]
        )

    shifts = (1, roles - 1, 2)
    order = (0,) + shifts
    wave_cols, place = call(
        begin_kernel,
        [jax.ShapeDtypeStruct((share, 128), bf16), jax.ShapeDtypeStruct((3, atoms), f32)],
        [wave, jnp.transpose(positions, (0, 2, 1, 3))[0]],
        scratch=[
            pltpu.VMEM((3, share), jnp.int32),
            pltpu.VMEM((3, 1, atoms), f32),
            pltpu.VMEM((128, 128), f32),
            pltpu.SemaphoreType.DMA((2,)),
        ],
        nbytes=1 << 19,
        spec=[HBM] * 2,
    )
    place_of = {0: place, **{d: from_role(place, d) for d in shifts}}
    rows_of = {0: rows}
    for d in shifts:
        rows_of[d] = from_role(rows, d)
    by_wave = call(
        tables_kernel,
        jax.ShapeDtypeStruct((2 * share, roles * atoms), bf16),
        [place_of[d] for d in order] + [wave_cols],
        scratch=[pltpu.VMEM((128, roles * atoms), f32), pltpu.VMEM((128, roles * atoms), bf16)],
        flops=40 * share * roles * atoms,
        nbytes=4 << 20,
    )
    norm = atom_total ** (-0.5)
    partner = [(i, i ^ 1) for i in range(columns)]
    same_core = [list(range(c, columns, 2)) for c in range(2)]
    sent, queries = call(
        functools.partial(send_kernel, norm),
        [jax.ShapeDtypeStruct((share, width), bf16), jax.ShapeDtypeStruct((roles * atoms, width), bf16)],
        [rows_of[d] for d in order] + [w_query, by_wave],
        flops=2 * share * roles * atoms * width,
        nbytes=3 << 20,
    )
    got = lax.ppermute(sent, "atoms", partner)
    own = call(
        functools.partial(own_kernel, norm),
        jax.ShapeDtypeStruct((share, width), f32),
        [queries, by_wave],
        flops=2 * share * roles * atoms * width,
        nbytes=2 << 20,
    )
    kept = call(
        keep_kernel,
        jax.ShapeDtypeStruct((share, width), bf16),
        [own, got],
        flops=share * width,
        nbytes=1 << 20,
    )
    by_atom = call(
        flip_kernel,
        jax.ShapeDtypeStruct((roles * atoms, 2 * share), bf16),
        [by_wave],
        nbytes=4 << 20,
    )
    chunks = (columns // 2, 2 * piece, width)
    mine = lax.all_to_all(kept.reshape(chunks), "atoms", 0, 0, axis_index_groups=same_core)
    copies = call(
        reduce_kernel,
        jax.ShapeDtypeStruct(chunks, bf16),
        [mine, wave, kgain[None, :]],
        flops=2 * share * width,
        nbytes=1 << 20,
    )
    half_own = lax.all_to_all(copies, "atoms", 0, 0, axis_index_groups=same_core).reshape(
        share, width
    )
    half_other = lax.ppermute(half_own, "atoms", partner)

    triple = (roles - 1, 0, 1)
    bundle = call(
        stack_kernel,
        jax.ShapeDtypeStruct((3, atoms + 32, width), bf16),
        [rows_of[d] for d in triple] + [place_of[d] for d in triple],
        scratch=[pltpu.VMEM((32, width), f32)],
        nbytes=1 << 20,
    )
    low, high = from_column(bundle, columns - 1), from_column(bundle, 1)
    table, cols, pairs, bias, row_at, filter_weight = call(
        prepare_kernel,
        [
            jax.ShapeDtypeStruct((9 * atoms * width // 128 + 16, 128), f32),
            jax.ShapeDtypeStruct((atoms, 4 * slots), bf16),
            jax.ShapeDtypeStruct((2 * w_rbf.shape[0], 2 * width), bf16),
            jax.ShapeDtypeStruct((1, 2 * width), f32),
            jax.ShapeDtypeStruct((slots, atoms), jnp.int32),
            jax.ShapeDtypeStruct((width, width), bf16),
        ],
        [rows_of[d] for d in triple]
        + [low, high]
        + [place_of[d] for d in triple]
        + [neighbours[0, 0], images[0, 0], w_in, w_rbf, b_rbf[None, :], w_filter],
        scratch=[pltpu.VMEM((8, 9 * atoms), f32), pltpu.VMEM((4 * slots, atoms), f32)],
        flops=2 * 9 * atoms * width * width,
        nbytes=4 << 20,
    )
    near = pltpu.VMEM((4 * atoms * width // 128, 128), f32)
    short = ()
    for i in range(2):
        short = (
            call(
                functools.partial(
                    short_kernel, i * slots // 2, slots // 2, slots ** (-0.5) if i else 1.0
                ),
                jax.ShapeDtypeStruct((atoms, width), f32),
                [cols, table, row_at, pairs, bias, filter_weight, *short],
                scratch=[near, near]
                + [pltpu.SMEM((8, atoms), jnp.int32)] * 2
                + [pltpu.SemaphoreType.DMA((2,))],
                flops=2 * slots * atoms * width * width,
                nbytes=4 << 20,
            ),
        )
    short = short[0]
    parts = call(
        ewald_kernel,
        [jax.ShapeDtypeStruct((atoms, width), bf16)] * roles,
        [by_atom, half_own, half_other],
        flops=2 * 2 * share * roles * atoms * width,
        nbytes=4 << 20,
    )
    back = [parts[0]] + [from_role(parts[1 + i], roles - d) for i, d in enumerate(shifts)]
    result = call(
        final_kernel,
        jax.ShapeDtypeStruct((atoms, width), bf16),
        [rows, short] + back + [w_out],
        flops=2 * atoms * width * width,
        nbytes=1 << 20,
    )
    return result[None, None]


def solution(mesh):
    in_specs = (
        P("role", "atoms", None, None),
        P("role", "atoms", None, None),
        P("role", "atoms", None, None),
        P("role", "atoms", None, None),
        P(),
        P(),
        P(),
        P(),
        P(),
        P(),
        P(),
        P(),
    )
    out_specs = P("role", "atoms", None, None)
    return jax.shard_map(block, mesh=mesh, in_specs=in_specs, out_specs=out_specs, check_vma=False)
```

```python
import functools
import math

import jax
import jax.numpy as jnp
from jax import lax
from jax.experimental import pallas as pl
from jax.experimental.pallas import tpu as pltpu
from jax.sharding import PartitionSpec as P


box_side = 1.0
soft_sq = 0.01
damping = 64.0
ewald_scale = 0.25
SINE = (3.1415820220239103, -5.167142791318864, 2.541898979237898, -0.5546360684015085)
COSINE = (
    0.9999999534655706,
    -4.934792858503339,
    4.058411910098915,
    -1.331880131184001,
    0.21969673041819898,
)
ZOOM = 16.0 * math.sqrt(math.log2(math.e))
VMEM = pl.BlockSpec(memory_space=pltpu.VMEM)
HBM = pl.BlockSpec(memory_space=pltpu.HBM)


def call(body, out, ins, scratch=(), flops=0, nbytes=0, trans=0, grant=16, spec=None):
    multiple = isinstance(out, (list, tuple))
    return pl.pallas_call(
        body,
        out_shape=out,
        in_specs=spec or [VMEM] * len(ins),
        out_specs=[VMEM] * len(out) if multiple else VMEM,
        scratch_shapes=list(scratch),
        compiler_params=pltpu.CompilerParams(vmem_limit_bytes=int(grant * (1 << 20))),
        cost_estimate=pl.CostEstimate(flops=flops, bytes_accessed=nbytes, transcendentals=trans),
    )(*ins)


def dot(left, right):
    return jnp.dot(left, right, preferred_element_type=jnp.float32)


def sine_cosine(turns):
    rest = turns - jnp.round(turns)
    square = rest * rest
    odd = SINE[-1]
    for coef in SINE[-2::-1]:
        odd = odd * square + coef
    even = COSINE[-1]
    for coef in COSINE[-2::-1]:
        even = even * square + coef
    half = odd * rest
    return 2.0 * (half * even), 1.0 - 2.0 * (half * half)


def begin_kernel(wave_hbm, place_hbm, cols, place_out, waves, place, flat, sems):
    share = cols.shape[0]
    first = pl.multiple_of(lax.axis_index("role") * share, 128)
    copies = [
        pltpu.make_async_copy(wave_hbm.at[:, pl.ds(first, share)], waves, sems.at[0]),
        pltpu.make_async_copy(place_hbm, place, sems.at[1]),
    ]
    for copy in copies:
        copy.start()
    flat[...] = jnp.zeros_like(flat)
    copies[0].wait()
    for i in range(share // 128):
        part = waves[:, i * 128 : (i + 1) * 128].astype(jnp.float32)
        for k in range(3):
            flat[3 * k : 3 * k + 3, :] = part
        cols[i * 128 : (i + 1) * 128, :] = flat[...].T.astype(jnp.bfloat16)
    copies[1].wait()
    for c in range(3):
        place_out[c : c + 1, :] = place[c]


def tables_kernel(*refs):
    pos_refs, (cols, by_wave, pos, parts) = refs[:4], refs[4:]
    atoms = pos_refs[0].shape[1]
    total = pos.shape[1]
    pos[...] = jnp.zeros_like(pos)
    for i, ref in enumerate(pos_refs):
        rest = ref[...]
        for k in range(3):
            rounded = rest.astype(jnp.bfloat16).astype(jnp.float32)
            pos[3 * k : 3 * k + 3, i * atoms : (i + 1) * atoms] = rounded
            rest = rest - rounded
    parts[...] = pos[...].astype(jnp.bfloat16)
    share = by_wave.shape[0] // 2
    step = 64

    def block(j, carry):
        waves = cols[pl.ds(pl.multiple_of(j * step, step), step), :]
        sine, cosine = sine_cosine(dot(waves, parts[...]))
        both = jnp.stack(
            [cosine.reshape(step // 8, 8, total), sine.reshape(step // 8, 8, total)], axis=1
        ).reshape(2 * step, total)
        part = pl.ds(pl.multiple_of(j * 2 * step, 2 * step), 2 * step)
        by_wave[part, :] = both.astype(jnp.bfloat16)
        return carry

    lax.fori_loop(0, share // step, block, 0)


def again_kernel(*refs):
    pos_refs, (wave_ref, by_atom, flat, pos, parts) = refs[:4], refs[4:]
    atoms = pos_refs[0].shape[1]
    columns = by_atom.shape[1]
    share = columns // 2
    first = pl.multiple_of(lax.axis_index("role") * share, 128)
    waves = wave_ref[:, pl.ds(first, share)].astype(jnp.float32)
    flat[...] = jnp.zeros_like(flat)
    pos[...] = jnp.zeros_like(pos)
    for k in range(3):
        flat[3 * k : 3 * k + 3, :] = waves
    pos[9:10, :] = jnp.ones((1, pos.shape[1]), jnp.float32)
    for i, ref in enumerate(pos_refs):
        rest = ref[...]
        for k in range(3):
            rounded = rest.astype(jnp.bfloat16).astype(jnp.float32)
            pos[3 * k : 3 * k + 3, i * atoms : (i + 1) * atoms] = rounded
            rest = rest - rounded
    for i in range(pos.shape[1] // 128):
        part = slice(i * 128, (i + 1) * 128)
        parts[part, :] = pos[:, part].T.astype(jnp.bfloat16)
    row = lax.broadcasted_iota(jnp.int32, (share, columns), 0)
    lane = lax.broadcasted_iota(jnp.int32, (share, columns), 1)
    pick = (row == (lane >> 4) * 8 + (lane & 7)).astype(jnp.float32).astype(jnp.bfloat16)
    spread = dot(flat[...].astype(jnp.bfloat16), pick)
    row = lax.broadcasted_iota(jnp.int32, spread.shape, 0)
    lane = lax.broadcasted_iota(jnp.int32, spread.shape, 1)
    spread = jnp.where((row == 9) & ((lane & 8) != 0), -0.25, spread).astype(jnp.bfloat16)
    step = 128

    def block(j, carry):
        part = pl.ds(pl.multiple_of(j * step, step), step)
        turns = dot(parts[part, :], spread)
        rest = turns - jnp.round(turns)
        square = rest * rest
        odd = SINE[-1]
        for coef in SINE[-2::-1]:
            odd = odd * square + coef
        half = odd * rest
        by_atom[part, :] = (1.0 - 2.0 * (half * half)).astype(jnp.bfloat16)
        return carry

    lax.fori_loop(0, pos.shape[1] // step, block, 0)


def core_half(size, other):
    core = lax.axis_index("atoms") & 1
    core = 1 - core if other else core
    return pl.ds(pl.multiple_of(core * size, size), size)


def send_kernel(scale, *refs):
    rows_refs, (wq_ref, table, out_ref, queries) = refs[:4], refs[4:]
    atoms = rows_refs[0].shape[0]
    weight = wq_ref[...]
    for i, rows in enumerate(rows_refs):
        queries[i * atoms : (i + 1) * atoms, :] = dot(rows[...], weight).astype(jnp.bfloat16)
    part = core_half(out_ref.shape[0], True)
    out_ref[...] = (dot(table[part, :], queries[...]) * scale).astype(jnp.bfloat16)


def own_kernel(scale, queries, table, out_ref):
    part = core_half(out_ref.shape[0], False)
    out_ref[...] = dot(table[part, :], queries[...]) * scale


def keep_kernel(own_ref, got_ref, out_ref):
    out_ref[...] = (own_ref[...] + got_ref[...].astype(jnp.float32)).astype(jnp.bfloat16)


def stack_kernel(*refs):
    rows_refs, pos_refs, (out_ref, parts) = refs[:3], refs[3:6], refs[6:]
    atoms = rows_refs[0].shape[0]
    parts[...] = jnp.zeros_like(parts)
    for i in range(3):
        out_ref[i, 0:atoms, :] = rows_refs[i][...]
        rest = pos_refs[i][...]
        for k in range(3):
            rounded = rest.astype(jnp.bfloat16).astype(jnp.float32)
            parts[8 * k : 8 * k + 3, :] = rounded
            rest = rest - rounded
        out_ref[i, atoms:, :] = parts[...].astype(jnp.bfloat16)


def reduce_kernel(mine_ref, wave_ref, kgain_ref, out_ref):
    chips, rows, width = mine_ref.shape
    piece = rows // 2
    share = 2 * chips * piece
    column = lax.axis_index("atoms")
    first = lax.axis_index("role") * share + ((column & 1) * chips + (column >> 1)) * piece
    start = pl.multiple_of((first // 128) * 128, 128)
    waves = wave_ref[:, pl.ds(start, 128)].astype(jnp.float32)
    squares = jnp.broadcast_to(jnp.sum(waves * waves, axis=0, keepdims=True), (piece, 128))
    lanes = lax.broadcasted_iota(jnp.int32, (piece, 128), 1)
    wanted = lax.broadcasted_iota(jnp.int32, (piece, 128), 0) + (first - start)
    square = jnp.sum(jnp.where(lanes == wanted, squares, 0.0), axis=1, keepdims=True)
    k_filter = ewald_scale * kgain_ref[...] * (jnp.exp(-square / damping) / square)
    total = jnp.sum(mine_ref[...].astype(jnp.float32), axis=0)
    filtered = total * jnp.concatenate([k_filter, k_filter], axis=0)
    out_ref[...] = jnp.broadcast_to(filtered.astype(jnp.bfloat16)[None], (chips, rows, width))


def ewald_kernel(table_ref, own_ref, other_ref, *out_refs):
    atoms, _ = out_refs[0].shape
    size = own_ref.shape[0]
    for i, out_ref in enumerate(out_refs):
        part = slice(i * atoms, (i + 1) * atoms)
        total = dot(table_ref[part, core_half(size, False)], own_ref[...])
        total = total + dot(table_ref[part, core_half(size, True)], other_ref[...])
        out_ref[...] = total.astype(jnp.bfloat16)


def final_kernel(rows_ref, short_ref, e0_ref, e1_ref, e2_ref, e3_ref, wout_ref, out_ref):
    total = short_ref[...]
    for ref in (e0_ref, e1_ref, e2_ref, e3_ref):
        total = total + ref[...].astype(jnp.float32)
    moved = dot(total.astype(jnp.bfloat16), wout_ref[...])
    out_ref[...] = (rows_ref[...].astype(jnp.float32) + moved).astype(jnp.bfloat16)


def prepare_kernel(
    r0, r1, r2, low_ref, high_ref, p0, p1, p2, slots_ref, images_ref, win_ref, wrbf_ref, brbf_ref, wf_ref,
    table, cols, row_at, wrbf_out, brbf_out, wf_out, pos, turned,
):
    width = wf_ref.shape[1]
    wrbf_out[...] = wrbf_ref[...]
    brbf_out[...] = brbf_ref[...]
    lane = 128
    halves = width // lane
    slots, atoms = slots_ref.shape
    weight = win_ref[...]
    own = (r0, r1, r2)
    for p in range(3):
        for q in range(3):
            brick = p * 3 + q
            if q == 1:
                rows, place = own[p][...], (p0, p1, p2)[p][...]
            else:
                ref = low_ref if q == 0 else high_ref
                rows = ref[p, 0:atoms, :]
                parts = ref[p, atoms:, :].astype(jnp.float32)
                place = (parts[0:3, :] + parts[8:11, :]) + parts[16:19, :]
            hidden = dot(rows, weight).astype(jnp.bfloat16).astype(jnp.float32)
            for h in range(halves):
                table[pl.ds(halves * brick * atoms + h, atoms, stride=halves), :] = hidden[
                    :, h * lane : (h + 1) * lane
                ]
            pos[0:3, brick * atoms : (brick + 1) * atoms] = place
    row_at[...] = slots_ref[...] * halves
    wf_out[...] = wf_ref[...]
    table[halves * 9 * atoms :, :] = jnp.zeros((table.shape[0] - halves * 9 * atoms, lane), jnp.float32)
    for half in range(atoms // lane):
        cut = slice(half * lane, (half + 1) * lane)
        index = slots_ref[:, cut]
        image = images_ref[:, cut]
        place = index & (lane - 1)
        group = index >> 7
        near = [jnp.zeros((slots, lane), jnp.float32) for _ in range(3)]
        for r in range(9 * atoms // lane):
            here = group == r
            for c in range(3):
                table = jnp.broadcast_to(pos[c : c + 1, r * lane : (r + 1) * lane], (slots, lane))
                taken = jnp.take_along_axis(table, place, axis=1, mode="promise_in_bounds")
                near[c] = jnp.where(here, taken, near[c])
        first = (image >= 9).astype(jnp.int32) + (image >= 18).astype(jnp.int32)
        inside = image - 9 * first
        second = (inside >= 3).astype(jnp.int32) + (inside >= 6).astype(jnp.int32)
        third = inside - 3 * second
        square = jnp.zeros((slots, lane), jnp.float32)
        for c, offset in enumerate((first, second, third)):
            delta = near[c] + (offset - 1).astype(jnp.float32) * box_side - p1[c : c + 1, cut]
            square = square + delta * delta
        rest = jnp.sqrt(square + soft_sq) * ZOOM
        for k in range(3):
            rounded = rest.astype(jnp.bfloat16).astype(jnp.float32)
            turned[k * slots : (k + 1) * slots, cut] = rounded
            rest = rest - rounded
        turned[3 * slots : 4 * slots, cut] = jnp.zeros((slots, lane), jnp.float32)
    cols[...] = turned[...].T.astype(jnp.bfloat16)


def short_kernel(start, count, scale, cols_ref, table, row_at, wrbf_ref, brbf_ref, wf_ref, *refs):
    lane = 128
    atoms = cols_ref.shape[0]
    slots = cols_ref.shape[1] // 4
    basis_count, width = wrbf_ref.shape
    halves = width // lane
    *before, out_ref, near_a, near_b, at_a, at_b, pairs, bias, sems = refs
    pairs[...] = jnp.zeros_like(pairs)
    pairs[0:basis_count, 0:width] = wrbf_ref[...]
    pairs[basis_count:, width:] = wrbf_ref[...]
    bias[:, 0:width] = brbf_ref[...] * math.log2(math.e)
    bias[:, width:] = brbf_ref[...] * math.log2(math.e)
    group = near_a.shape[0] // (halves * atoms)
    ahead = at_a.shape[0]
    wide_lanes = group // 2 * lane
    out_ref[...] = before[0][...] if before else jnp.zeros_like(out_ref)
    row = lax.broadcasted_iota(jnp.int32, (lane, wide_lanes), 0)
    column = lax.broadcasted_iota(jnp.int32, (lane, wide_lanes), 1)
    source = jnp.where(row < 3 * slots, (row & (slots - 1)) - (column >> 6), -lane)
    centers = (
        (lax.broadcasted_iota(jnp.int32, (1, lane), 1) & (basis_count - 1)).astype(jnp.float32)
        * (4.0 / (basis_count - 1))
        * ZOOM
    )

    def fetch(first, buffer, sem):
        rows = pl.ds(pl.multiple_of(first, ahead), ahead)
        return pltpu.make_async_copy(row_at.at[rows, :], buffer, sem)

    def one_group(first, buffer, offset, near):
        for i in range(group):
            for k in range(atoms):
                to = (i * atoms + k) * halves
                near[to : to + halves, :] = table[pl.ds(buffer[offset + i, k], halves), :]
        select = (source == first).astype(jnp.float32).astype(jnp.bfloat16)
        wide = dot(cols_ref[...], select)
        inner = []
        for p in range(group // 2):
            offset = wide[:, p * lane : (p + 1) * lane] - centers
            basis = jnp.exp2(-(offset * offset)).astype(jnp.bfloat16)
            value = dot(basis, pairs[...]) * math.log2(math.e) + bias[...]
            both = (jnp.log(1.0 + jnp.exp2(value)) - math.log(2.0)).astype(jnp.bfloat16)
            inner += [both[:, :width], both[:, width:]]
        filters = dot(jnp.concatenate(inner, axis=0), wf_ref[...])
        for h in range(halves):
            cut = slice(h * lane, (h + 1) * lane)
            total = out_ref[:, cut]
            for i in range(group):
                gathered = near[pl.ds(i * atoms * halves + h, atoms, stride=halves), :]
                total = total + filters[i * atoms : (i + 1) * atoms, cut] * gathered
            out_ref[:, cut] = total

    def both_groups(first, buffer):
        one_group(first, buffer, 0, near_a)
        one_group(first + group, buffer, group, near_b)

    fetch(start, at_a, sems.at[0]).start()

    def body(j, carry):
        first = start + 2 * ahead * j
        fetch(first, at_a, sems.at[0]).wait()
        fetch(first + ahead, at_b, sems.at[1]).start()
        both_groups(first, at_a)
        fetch(first + ahead, at_b, sems.at[1]).wait()

        @pl.when(first + 2 * ahead < start + count)
        def _():
            fetch(first + 2 * ahead, at_a, sems.at[0]).start()

        both_groups(first + ahead, at_b)
        return carry

    lax.fori_loop(0, count // (2 * ahead), body, 0)
    out_ref[...] = out_ref[...] * scale


def block(
    features,
    positions,
    neighbours,
    images,
    wave,
    kgain,
    w_in,
    w_query,
    w_rbf,
    b_rbf,
    w_filter,
    w_out,
):
    f32, bf16 = jnp.float32, jnp.bfloat16
    rows = features[0, 0]
    atoms, width = rows.shape
    slots = neighbours.shape[2]
    roles = lax.axis_size("role")
    columns = lax.axis_size("atoms")
    atom_total = atoms * roles * columns
    waves = wave.shape[1]
    share = waves // roles
    piece = share // columns

    def from_role(block, shift):
        return lax.ppermute(block, "role", [((i + shift) % roles, i) for i in range(roles)])

    def from_column(block, shift):
        return lax.ppermute(
            block, "atoms", [((i + shift) % columns, i) for i in range(columns)]
        )

    shifts = (1, roles - 1, 2)
    order = (0,) + shifts
    wave_cols, place = call(
        begin_kernel,
        [jax.ShapeDtypeStruct((share, 128), bf16), jax.ShapeDtypeStruct((3, atoms), f32)],
        [wave, jnp.transpose(positions, (0, 2, 1, 3))[0]],
        scratch=[
            pltpu.VMEM((3, share), jnp.int32),
            pltpu.VMEM((3, 1, atoms), f32),
            pltpu.VMEM((128, 128), f32),
            pltpu.SemaphoreType.DMA((2,)),
        ],
        nbytes=1 << 19,
        spec=[HBM] * 2,
    )
    place_of = {0: place, **{d: from_role(place, d) for d in shifts}}
    rows_of = {0: rows}
    for d in shifts:
        rows_of[d] = from_role(rows, d)
    by_wave = call(
        tables_kernel,
        jax.ShapeDtypeStruct((2 * share, roles * atoms), bf16),
        [place_of[d] for d in order] + [wave_cols],
        scratch=[pltpu.VMEM((128, roles * atoms), f32), pltpu.VMEM((128, roles * atoms), bf16)],
        flops=40 * share * roles * atoms,
        nbytes=4 << 20,
    )
    norm = atom_total ** (-0.5)
    partner = [(i, i ^ 1) for i in range(columns)]
    same_core = [list(range(c, columns, 2)) for c in range(2)]
    sent, queries = call(
        functools.partial(send_kernel, norm),
        [jax.ShapeDtypeStruct((share, width), bf16), jax.ShapeDtypeStruct((roles * atoms, width), bf16)],
        [rows_of[d] for d in order] + [w_query, by_wave],
        flops=2 * share * roles * atoms * width,
        nbytes=3 << 20,
    )
    got = lax.ppermute(sent, "atoms", partner)
    own = call(
        functools.partial(own_kernel, norm),
        jax.ShapeDtypeStruct((share, width), f32),
        [queries, by_wave],
        flops=2 * share * roles * atoms * width,
        nbytes=2 << 20,
    )
    kept = call(
        keep_kernel,
        jax.ShapeDtypeStruct((share, width), bf16),
        [own, got],
        flops=share * width,
        nbytes=1 << 20,
    )
    by_atom = call(
        again_kernel,
        jax.ShapeDtypeStruct((roles * atoms, 2 * share), bf16),
        [place_of[d] for d in order] + [wave],
        scratch=[
            pltpu.VMEM((128, share), f32),
            pltpu.VMEM((128, roles * atoms), f32),
            pltpu.VMEM((roles * atoms, 128), bf16),
        ],
        flops=40 * share * roles * atoms,
        nbytes=2 << 20,
    )
    chunks = (columns // 2, 2 * piece, width)
    mine = lax.all_to_all(kept.reshape(chunks), "atoms", 0, 0, axis_index_groups=same_core)
    copies = call(
        reduce_kernel,
        jax.ShapeDtypeStruct(chunks, bf16),
        [mine, wave, kgain[None, :]],
        flops=2 * share * width,
        nbytes=1 << 20,
    )
    half_own = lax.all_to_all(copies, "atoms", 0, 0, axis_index_groups=same_core).reshape(
        share, width
    )
    half_other = lax.ppermute(half_own, "atoms", partner)

    triple = (roles - 1, 0, 1)
    bundle = call(
        stack_kernel,
        jax.ShapeDtypeStruct((3, atoms + 32, width), bf16),
        [rows_of[d] for d in triple] + [place_of[d] for d in triple],
        scratch=[pltpu.VMEM((32, width), f32)],
        nbytes=1 << 20,
    )
    low, high = from_column(bundle, columns - 1), from_column(bundle, 1)
    table, cols, row_at, *held = call(
        prepare_kernel,
        [
            jax.ShapeDtypeStruct((9 * atoms * width // 128 + 16, 128), f32),
            jax.ShapeDtypeStruct((atoms, 4 * slots), bf16),
            jax.ShapeDtypeStruct((slots, atoms), jnp.int32),
            jax.ShapeDtypeStruct(w_rbf.shape, bf16),
            jax.ShapeDtypeStruct((1, width), f32),
            jax.ShapeDtypeStruct((width, width), bf16),
        ],
        [rows_of[d] for d in triple]
        + [low, high]
        + [place_of[d] for d in triple]
        + [neighbours[0, 0], images[0, 0], w_in, w_rbf, b_rbf[None, :], w_filter],
        scratch=[pltpu.VMEM((8, 9 * atoms), f32), pltpu.VMEM((4 * slots, atoms), f32)],
        flops=2 * 9 * atoms * width * width,
        nbytes=4 << 20,
    )
    near = pltpu.VMEM((4 * atoms * width // 128, 128), f32)
    short = ()
    for i in range(2):
        short = (
            call(
                functools.partial(
                    short_kernel, i * slots // 2, slots // 2, slots ** (-0.5) if i else 1.0
                ),
                jax.ShapeDtypeStruct((atoms, width), f32),
                [cols, table, row_at]
                + ([w_rbf, b_rbf[None, :], w_filter] if i else held)
                + [*short],
                scratch=[near, near]
                + [pltpu.SMEM((8, atoms), jnp.int32)] * 2
                + [
                    pltpu.VMEM((2 * w_rbf.shape[0], 2 * width), bf16),
                    pltpu.VMEM((1, 2 * width), f32),
                ]
                + [pltpu.SemaphoreType.DMA((2,))],
                flops=2 * slots * atoms * width * width,
                nbytes=4 << 20,
            ),
        )
    short = short[0]
    parts = call(
        ewald_kernel,
        [jax.ShapeDtypeStruct((atoms, width), bf16)] * roles,
        [by_atom, half_own, half_other],
        flops=2 * 2 * share * roles * atoms * width,
        nbytes=4 << 20,
    )
    back = [parts[0]] + [from_role(parts[1 + i], roles - d) for i, d in enumerate(shifts)]
    result = call(
        final_kernel,
        jax.ShapeDtypeStruct((atoms, width), bf16),
        [rows, short] + back + [w_out],
        flops=2 * atoms * width * width,
        nbytes=1 << 20,
    )
    return result[None, None]


def solution(mesh):
    in_specs = (
        P("role", "atoms", None, None),
        P("role", "atoms", None, None),
        P("role", "atoms", None, None),
        P("role", "atoms", None, None),
        P(),
        P(),
        P(),
        P(),
        P(),
        P(),
        P(),
        P(),
    )
    out_specs = P("role", "atoms", None, None)
    return jax.shard_map(block, mesh=mesh, in_specs=in_specs, out_specs=out_specs, check_vma=False)
```

```python
import functools
import math

import jax
import jax.numpy as jnp
from jax import lax
from jax.experimental import pallas as pl
from jax.experimental.pallas import tpu as pltpu
from jax.sharding import PartitionSpec as P


box_side = 1.0
soft_sq = 0.01
damping = 64.0
ewald_scale = 0.25
SINE = (3.1415820220239103, -5.167142791318864, 2.541898979237898, -0.5546360684015085)
COSINE = (
    0.9999999534655706,
    -4.934792858503339,
    4.058411910098915,
    -1.331880131184001,
    0.21969673041819898,
)
ZOOM = 16.0 * math.sqrt(math.log2(math.e))
VMEM = pl.BlockSpec(memory_space=pltpu.VMEM)
HBM = pl.BlockSpec(memory_space=pltpu.HBM)


def call(body, out, ins, scratch=(), flops=0, nbytes=0, trans=0, grant=16, spec=None):
    multiple = isinstance(out, (list, tuple))
    return pl.pallas_call(
        body,
        out_shape=out,
        in_specs=spec or [VMEM] * len(ins),
        out_specs=[VMEM] * len(out) if multiple else VMEM,
        scratch_shapes=list(scratch),
        compiler_params=pltpu.CompilerParams(vmem_limit_bytes=int(grant * (1 << 20))),
        cost_estimate=pl.CostEstimate(flops=flops, bytes_accessed=nbytes, transcendentals=trans),
    )(*ins)


def dot(left, right):
    return jnp.dot(left, right, preferred_element_type=jnp.float32)


def sine_cosine(turns):
    rest = turns - jnp.round(turns)
    square = rest * rest
    odd = SINE[-1]
    for coef in SINE[-2::-1]:
        odd = odd * square + coef
    even = COSINE[-1]
    for coef in COSINE[-2::-1]:
        even = even * square + coef
    half = odd * rest
    return 2.0 * (half * even), 1.0 - 2.0 * (half * half)


def begin_kernel(wave_hbm, place_hbm, cols, place_out, waves, place, flat, sems):
    share = cols.shape[0]
    first = pl.multiple_of(lax.axis_index("role") * share, 128)
    copies = [
        pltpu.make_async_copy(wave_hbm.at[:, pl.ds(first, share)], waves, sems.at[0]),
        pltpu.make_async_copy(place_hbm, place, sems.at[1]),
    ]
    for copy in copies:
        copy.start()
    flat[...] = jnp.zeros_like(flat)
    copies[0].wait()
    for i in range(share // 128):
        part = waves[:, i * 128 : (i + 1) * 128].astype(jnp.float32)
        for k in range(3):
            flat[3 * k : 3 * k + 3, :] = part
        cols[i * 128 : (i + 1) * 128, :] = flat[...].T.astype(jnp.bfloat16)
    copies[1].wait()
    for c in range(3):
        place_out[c : c + 1, :] = place[c]


def tables_kernel(*refs):
    pos_refs, (cols, by_wave, pos, parts) = refs[:4], refs[4:]
    atoms = pos_refs[0].shape[1]
    total = pos.shape[1]
    pos[...] = jnp.zeros_like(pos)
    for i, ref in enumerate(pos_refs):
        rest = ref[...]
        for k in range(3):
            rounded = rest.astype(jnp.bfloat16).astype(jnp.float32)
            pos[3 * k : 3 * k + 3, i * atoms : (i + 1) * atoms] = rounded
            rest = rest - rounded
    parts[...] = pos[...].astype(jnp.bfloat16)
    share = by_wave.shape[0] // 2
    step = 64

    def block(j, carry):
        waves = cols[pl.ds(pl.multiple_of(j * step, step), step), :]
        sine, cosine = sine_cosine(dot(waves, parts[...]))
        both = jnp.stack(
            [cosine.reshape(step // 8, 8, total), sine.reshape(step // 8, 8, total)], axis=1
        ).reshape(2 * step, total)
        part = pl.ds(pl.multiple_of(j * 2 * step, 2 * step), 2 * step)
        by_wave[part, :] = both.astype(jnp.bfloat16)
        return carry

    lax.fori_loop(0, share // step, block, 0)


def again_kernel(*refs):
    pos_refs, (wave_ref, by_atom, flat, pos, parts) = refs[:4], refs[4:]
    atoms = pos_refs[0].shape[1]
    columns = by_atom.shape[1]
    share = columns // 2
    first = pl.multiple_of(lax.axis_index("role") * share, 128)
    waves = wave_ref[:, pl.ds(first, share)].astype(jnp.float32)
    flat[...] = jnp.zeros_like(flat)
    pos[...] = jnp.zeros_like(pos)
    for k in range(3):
        flat[3 * k : 3 * k + 3, :] = waves
    pos[9:10, :] = jnp.ones((1, pos.shape[1]), jnp.float32)
    for i, ref in enumerate(pos_refs):
        rest = ref[...]
        for k in range(3):
            rounded = rest.astype(jnp.bfloat16).astype(jnp.float32)
            pos[3 * k : 3 * k + 3, i * atoms : (i + 1) * atoms] = rounded
            rest = rest - rounded
    for i in range(pos.shape[1] // 128):
        part = slice(i * 128, (i + 1) * 128)
        parts[part, :] = pos[:, part].T.astype(jnp.bfloat16)
    row = lax.broadcasted_iota(jnp.int32, (share, columns), 0)
    lane = lax.broadcasted_iota(jnp.int32, (share, columns), 1)
    pick = (row == (lane >> 4) * 8 + (lane & 7)).astype(jnp.float32).astype(jnp.bfloat16)
    spread = dot(flat[...].astype(jnp.bfloat16), pick)
    row = lax.broadcasted_iota(jnp.int32, spread.shape, 0)
    lane = lax.broadcasted_iota(jnp.int32, spread.shape, 1)
    spread = jnp.where((row == 9) & ((lane & 8) != 0), -0.25, spread).astype(jnp.bfloat16)
    step = 128

    def block(j, carry):
        part = pl.ds(pl.multiple_of(j * step, step), step)
        turns = dot(parts[part, :], spread)
        rest = turns - jnp.round(turns)
        square = rest * rest
        odd = SINE[-1]
        for coef in SINE[-2::-1]:
            odd = odd * square + coef
        half = odd * rest
        by_atom[part, :] = (1.0 - 2.0 * (half * half)).astype(jnp.bfloat16)
        return carry

    lax.fori_loop(0, pos.shape[1] // step, block, 0)


def core_half(size, other):
    core = lax.axis_index("atoms") & 1
    core = 1 - core if other else core
    return pl.ds(pl.multiple_of(core * size, size), size)


def send_kernel(scale, *refs):
    rows_refs, (wq_ref, table, out_ref, queries) = refs[:4], refs[4:]
    atoms = rows_refs[0].shape[0]
    weight = wq_ref[...]
    for i, rows in enumerate(rows_refs):
        queries[i * atoms : (i + 1) * atoms, :] = dot(rows[...], weight).astype(jnp.bfloat16)
    part = core_half(out_ref.shape[0], True)
    out_ref[...] = (dot(table[part, :], queries[...]) * scale).astype(jnp.bfloat16)


def own_kernel(scale, queries, table, out_ref):
    part = core_half(out_ref.shape[0], False)
    out_ref[...] = dot(table[part, :], queries[...]) * scale


def keep_kernel(own_ref, got_ref, out_ref):
    out_ref[...] = (own_ref[...] + got_ref[...].astype(jnp.float32)).astype(jnp.bfloat16)


def stack_kernel(*refs):
    rows_refs, pos_refs, (out_ref, parts) = refs[:3], refs[3:6], refs[6:]
    atoms = rows_refs[0].shape[0]
    parts[...] = jnp.zeros_like(parts)
    for i in range(3):
        out_ref[i, 0:atoms, :] = rows_refs[i][...]
        rest = pos_refs[i][...]
        for k in range(3):
            rounded = rest.astype(jnp.bfloat16).astype(jnp.float32)
            parts[8 * k : 8 * k + 3, :] = rounded
            rest = rest - rounded
        out_ref[i, atoms:, :] = parts[...].astype(jnp.bfloat16)


def reduce_kernel(mine_ref, wave_ref, kgain_ref, out_ref):
    chips, rows, width = mine_ref.shape
    piece = rows // 2
    share = 2 * chips * piece
    column = lax.axis_index("atoms")
    first = lax.axis_index("role") * share + ((column & 1) * chips + (column >> 1)) * piece
    start = pl.multiple_of((first // 128) * 128, 128)
    waves = wave_ref[:, pl.ds(start, 128)].astype(jnp.float32)
    squares = jnp.broadcast_to(jnp.sum(waves * waves, axis=0, keepdims=True), (piece, 128))
    lanes = lax.broadcasted_iota(jnp.int32, (piece, 128), 1)
    wanted = lax.broadcasted_iota(jnp.int32, (piece, 128), 0) + (first - start)
    square = jnp.sum(jnp.where(lanes == wanted, squares, 0.0), axis=1, keepdims=True)
    k_filter = ewald_scale * kgain_ref[...] * (jnp.exp(-square / damping) / square)
    total = jnp.sum(mine_ref[...].astype(jnp.float32), axis=0)
    filtered = total * jnp.concatenate([k_filter, k_filter], axis=0)
    out_ref[...] = jnp.broadcast_to(filtered.astype(jnp.bfloat16)[None], (chips, rows, width))


def ewald_kernel(table_ref, own_ref, other_ref, *out_refs):
    atoms, _ = out_refs[0].shape
    size = own_ref.shape[0]
    for i, out_ref in enumerate(out_refs):
        part = slice(i * atoms, (i + 1) * atoms)
        total = dot(table_ref[part, core_half(size, False)], own_ref[...])
        total = total + dot(table_ref[part, core_half(size, True)], other_ref[...])
        out_ref[...] = total.astype(jnp.bfloat16)


def final_kernel(rows_ref, short_ref, e0_ref, e1_ref, e2_ref, e3_ref, wout_ref, out_ref):
    total = short_ref[...]
    for ref in (e0_ref, e1_ref, e2_ref, e3_ref):
        total = total + ref[...].astype(jnp.float32)
    moved = dot(total.astype(jnp.bfloat16), wout_ref[...])
    out_ref[...] = (rows_ref[...].astype(jnp.float32) + moved).astype(jnp.bfloat16)


def prepare_kernel(
    r0, r1, r2, low_ref, high_ref, p0, p1, p2, slots_ref, images_ref, win_ref, wrbf_ref, brbf_ref, wf_ref,
    table, cols, row_at, wrbf_out, brbf_out, wf_out, pos, turned,
):
    width = wf_ref.shape[1]
    wrbf_out[...] = wrbf_ref[...]
    brbf_out[...] = brbf_ref[...]
    lane = 128
    halves = width // lane
    slots, atoms = slots_ref.shape
    weight = win_ref[...]
    own = (r0, r1, r2)
    for p in range(3):
        for q in range(3):
            brick = p * 3 + q
            if q == 1:
                rows, place = own[p][...], (p0, p1, p2)[p][...]
            else:
                ref = low_ref if q == 0 else high_ref
                rows = ref[p, 0:atoms, :]
                parts = ref[p, atoms:, :].astype(jnp.float32)
                place = (parts[0:3, :] + parts[8:11, :]) + parts[16:19, :]
            hidden = dot(rows, weight).astype(jnp.bfloat16).astype(jnp.float32)
            for h in range(halves):
                table[pl.ds(halves * brick * atoms + h, atoms, stride=halves), :] = hidden[
                    :, h * lane : (h + 1) * lane
                ]
            pos[0:3, brick * atoms : (brick + 1) * atoms] = place
    row_at[...] = slots_ref[...] * halves
    wf_out[...] = wf_ref[...]
    table[halves * 9 * atoms :, :] = jnp.zeros((table.shape[0] - halves * 9 * atoms, lane), jnp.float32)
    for half in range(atoms // lane):
        cut = slice(half * lane, (half + 1) * lane)
        index = slots_ref[:, cut]
        image = images_ref[:, cut]
        place = index & (lane - 1)
        group = index >> 7
        near = [jnp.zeros((slots, lane), jnp.float32) for _ in range(3)]
        for r in range(9 * atoms // lane):
            here = group == r
            for c in range(3):
                table = jnp.broadcast_to(pos[c : c + 1, r * lane : (r + 1) * lane], (slots, lane))
                taken = jnp.take_along_axis(table, place, axis=1, mode="promise_in_bounds")
                near[c] = jnp.where(here, taken, near[c])
        first = (image >= 9).astype(jnp.int32) + (image >= 18).astype(jnp.int32)
        inside = image - 9 * first
        second = (inside >= 3).astype(jnp.int32) + (inside >= 6).astype(jnp.int32)
        third = inside - 3 * second
        square = jnp.zeros((slots, lane), jnp.float32)
        for c, offset in enumerate((first, second, third)):
            delta = near[c] + (offset - 1).astype(jnp.float32) * box_side - p1[c : c + 1, cut]
            square = square + delta * delta
        rest = jnp.sqrt(square + soft_sq) * ZOOM
        for k in range(3):
            rounded = rest.astype(jnp.bfloat16).astype(jnp.float32)
            turned[k * slots : (k + 1) * slots, cut] = rounded
            rest = rest - rounded
        turned[3 * slots : 4 * slots, cut] = jnp.zeros((slots, lane), jnp.float32)
    cols[...] = turned[...].T.astype(jnp.bfloat16)


def short_kernel(start, count, scale, cols_ref, table, row_at, wrbf_ref, brbf_ref, wf_ref, *refs):
    copy = pltpu.make_async_copy(row_at.at[start : start + count, :], refs[-4], refs[-1])
    copy.start()
    lane = 128
    atoms = cols_ref.shape[0]
    slots = cols_ref.shape[1] // 4
    basis_count, width = wrbf_ref.shape
    halves = width // lane
    *before, out_ref, near_a, near_b, near_at, pairs, bias, sem = refs
    pairs[...] = jnp.zeros_like(pairs)
    pairs[0:basis_count, 0:width] = wrbf_ref[...]
    pairs[basis_count:, width:] = wrbf_ref[...]
    bias[:, 0:width] = brbf_ref[...] * math.log2(math.e)
    bias[:, width:] = brbf_ref[...] * math.log2(math.e)
    group = near_a.shape[0] // (halves * atoms)
    wide_lanes = group // 2 * lane
    out_ref[...] = before[0][...] if before else jnp.zeros_like(out_ref)
    row = lax.broadcasted_iota(jnp.int32, (lane, wide_lanes), 0)
    column = lax.broadcasted_iota(jnp.int32, (lane, wide_lanes), 1)
    source = jnp.where(row < 3 * slots, (row & (slots - 1)) - (column >> 6), -lane)
    centers = (
        (lax.broadcasted_iota(jnp.int32, (1, lane), 1) & (basis_count - 1)).astype(jnp.float32)
        * (4.0 / (basis_count - 1))
        * ZOOM
    )

    def gather(i, near):
        for k in range(group * atoms):
            row = near_at[group * i + k // atoms, k % atoms]
            near[k * halves : (k + 1) * halves, :] = table[pl.ds(row, halves), :]

    def filters_of(i):
        select = (source == start + group * i).astype(jnp.float32).astype(jnp.bfloat16)
        wide = dot(cols_ref[...], select)
        inner = []
        for p in range(group // 2):
            offset = wide[:, p * lane : (p + 1) * lane] - centers
            basis = jnp.exp2(-(offset * offset)).astype(jnp.bfloat16)
            value = dot(basis, pairs[...]) * math.log2(math.e) + bias[...]
            both = (jnp.log(1.0 + jnp.exp2(value)) - math.log(2.0)).astype(jnp.bfloat16)
            inner += [both[:, :width], both[:, width:]]
        return dot(jnp.concatenate(inner, axis=0), wf_ref[...])

    def add(filters, near):
        for h in range(halves):
            cut = slice(h * lane, (h + 1) * lane)
            total = out_ref[:, cut]
            for i in range(group):
                gathered = near[pl.ds(i * atoms * halves + h, atoms, stride=halves), :]
                total = total + filters[i * atoms : (i + 1) * atoms, cut] * gathered
            out_ref[:, cut] = total

    filters = filters_of(0)
    copy.wait()
    for i in range(count // group):
        near = (near_a, near_b)[i % 2]
        gather(i, near)
        following = filters_of(i + 1) if group * (i + 1) < count else None
        add(filters, near)
        filters = following
    out_ref[...] = out_ref[...] * scale


def block(
    features,
    positions,
    neighbours,
    images,
    wave,
    kgain,
    w_in,
    w_query,
    w_rbf,
    b_rbf,
    w_filter,
    w_out,
):
    f32, bf16 = jnp.float32, jnp.bfloat16
    rows = features[0, 0]
    atoms, width = rows.shape
    slots = neighbours.shape[2]
    roles = lax.axis_size("role")
    columns = lax.axis_size("atoms")
    atom_total = atoms * roles * columns
    waves = wave.shape[1]
    share = waves // roles
    piece = share // columns

    def from_role(block, shift):
        return lax.ppermute(block, "role", [((i + shift) % roles, i) for i in range(roles)])

    def from_column(block, shift):
        return lax.ppermute(
            block, "atoms", [((i + shift) % columns, i) for i in range(columns)]
        )

    shifts = (1, roles - 1, 2)
    order = (0,) + shifts
    wave_cols, place = call(
        begin_kernel,
        [jax.ShapeDtypeStruct((share, 128), bf16), jax.ShapeDtypeStruct((3, atoms), f32)],
        [wave, jnp.transpose(positions, (0, 2, 1, 3))[0]],
        scratch=[
            pltpu.VMEM((3, share), jnp.int32),
            pltpu.VMEM((3, 1, atoms), f32),
            pltpu.VMEM((128, 128), f32),
            pltpu.SemaphoreType.DMA((2,)),
        ],
        nbytes=1 << 19,
        spec=[HBM] * 2,
    )
    place_of = {0: place, **{d: from_role(place, d) for d in shifts}}
    rows_of = {0: rows}
    for d in shifts:
        rows_of[d] = from_role(rows, d)
    by_wave = call(
        tables_kernel,
        jax.ShapeDtypeStruct((2 * share, roles * atoms), bf16),
        [place_of[d] for d in order] + [wave_cols],
        scratch=[pltpu.VMEM((128, roles * atoms), f32), pltpu.VMEM((128, roles * atoms), bf16)],
        flops=40 * share * roles * atoms,
        nbytes=4 << 20,
    )
    norm = atom_total ** (-0.5)
    partner = [(i, i ^ 1) for i in range(columns)]
    same_core = [list(range(c, columns, 2)) for c in range(2)]
    sent, queries = call(
        functools.partial(send_kernel, norm),
        [jax.ShapeDtypeStruct((share, width), bf16), jax.ShapeDtypeStruct((roles * atoms, width), bf16)],
        [rows_of[d] for d in order] + [w_query, by_wave],
        flops=2 * share * roles * atoms * width,
        nbytes=3 << 20,
    )
    got = lax.ppermute(sent, "atoms", partner)
    own = call(
        functools.partial(own_kernel, norm),
        jax.ShapeDtypeStruct((share, width), f32),
        [queries, by_wave],
        flops=2 * share * roles * atoms * width,
        nbytes=2 << 20,
    )
    kept = call(
        keep_kernel,
        jax.ShapeDtypeStruct((share, width), bf16),
        [own, got],
        flops=share * width,
        nbytes=1 << 20,
    )
    by_atom = call(
        again_kernel,
        jax.ShapeDtypeStruct((roles * atoms, 2 * share), bf16),
        [place_of[d] for d in order] + [wave],
        scratch=[
            pltpu.VMEM((128, share), f32),
            pltpu.VMEM((128, roles * atoms), f32),
            pltpu.VMEM((roles * atoms, 128), bf16),
        ],
        flops=40 * share * roles * atoms,
        nbytes=2 << 20,
    )
    chunks = (columns // 2, 2 * piece, width)
    mine = lax.all_to_all(kept.reshape(chunks), "atoms", 0, 0, axis_index_groups=same_core)
    copies = call(
        reduce_kernel,
        jax.ShapeDtypeStruct(chunks, bf16),
        [mine, wave, kgain[None, :]],
        flops=2 * share * width,
        nbytes=1 << 20,
    )
    half_own = lax.all_to_all(copies, "atoms", 0, 0, axis_index_groups=same_core).reshape(
        share, width
    )
    half_other = lax.ppermute(half_own, "atoms", partner)

    triple = (roles - 1, 0, 1)
    bundle = call(
        stack_kernel,
        jax.ShapeDtypeStruct((3, atoms + 32, width), bf16),
        [rows_of[d] for d in triple] + [place_of[d] for d in triple],
        scratch=[pltpu.VMEM((32, width), f32)],
        nbytes=1 << 20,
    )
    low, high = from_column(bundle, columns - 1), from_column(bundle, 1)
    table, cols, row_at, *held = call(
        prepare_kernel,
        [
            jax.ShapeDtypeStruct((9 * atoms * width // 128 + 16, 128), f32),
            jax.ShapeDtypeStruct((atoms, 4 * slots), bf16),
            jax.ShapeDtypeStruct((slots, atoms), jnp.int32),
            jax.ShapeDtypeStruct(w_rbf.shape, bf16),
            jax.ShapeDtypeStruct((1, width), f32),
            jax.ShapeDtypeStruct((width, width), bf16),
        ],
        [rows_of[d] for d in triple]
        + [low, high]
        + [place_of[d] for d in triple]
        + [neighbours[0, 0], images[0, 0], w_in, w_rbf, b_rbf[None, :], w_filter],
        scratch=[pltpu.VMEM((8, 9 * atoms), f32), pltpu.VMEM((4 * slots, atoms), f32)],
        flops=2 * 9 * atoms * width * width,
        nbytes=4 << 20,
    )
    near = pltpu.VMEM((2 * atoms * width // 128, 128), f32)
    short = ()
    for i in range(2):
        short = (
            call(
                functools.partial(
                    short_kernel, i * slots // 2, slots // 2, slots ** (-0.5) if i else 1.0
                ),
                jax.ShapeDtypeStruct((atoms, width), f32),
                [cols, table, row_at]
                + ([w_rbf, b_rbf[None, :], w_filter] if i else held)
                + [*short],
                scratch=[near, near]
                + [pltpu.SMEM((slots // 2, atoms), jnp.int32)]
                + [
                    pltpu.VMEM((2 * w_rbf.shape[0], 2 * width), bf16),
                    pltpu.VMEM((1, 2 * width), f32),
                ]
                + [pltpu.SemaphoreType.DMA],
                flops=2 * slots * atoms * width * width,
                nbytes=4 << 20,
            ),
        )
    short = short[0]
    parts = call(
        ewald_kernel,
        [jax.ShapeDtypeStruct((atoms, width), bf16)] * roles,
        [by_atom, half_own, half_other],
        flops=2 * 2 * share * roles * atoms * width,
        nbytes=4 << 20,
    )
    back = [parts[0]] + [from_role(parts[1 + i], roles - d) for i, d in enumerate(shifts)]
    result = call(
        final_kernel,
        jax.ShapeDtypeStruct((atoms, width), bf16),
        [rows, short] + back + [w_out],
        flops=2 * atoms * width * width,
        nbytes=1 << 20,
    )
    return result[None, None]


def solution(mesh):
    in_specs = (
        P("role", "atoms", None, None),
        P("role", "atoms", None, None),
        P("role", "atoms", None, None),
        P("role", "atoms", None, None),
        P(),
        P(),
        P(),
        P(),
        P(),
        P(),
        P(),
        P(),
    )
    out_specs = P("role", "atoms", None, None)
    return jax.shard_map(block, mesh=mesh, in_specs=in_specs, out_specs=out_specs, check_vma=False)
```
